512 devices in a mesh: leaf: 128 (over z, y, core), rhs: 4 (over x).
Axes of the slice: x: 4, y: 8, z: 8, core: 2. Of those that a mesh axis runs over, the one named last changes fastest.
Arguments:
- leaf_rhs: float32 [2, 64, 65536], P(None, 'rhs', 'leaf'), may hold values from -6 to 6
- sep_rhs: float32 [2, 64, 7, 1024], P(None, 'rhs', None, 'leaf'), may hold values from -6 to 6
- leaf_inv: bfloat16 [2, 512, 65536], P(None, 'rhs', 'leaf'), may hold values from -0.1875 to 0.1875
- leaf_low: bfloat16 [2, 512, 1024], P(None, None, 'leaf'), may hold values from -0.1875 to 0.1875
- sep_inv: bfloat16 [2, 8, 260096], P(None, None, 'leaf'), as said below
- sep_low: bfloat16 [2, 8, 129024], P(None, None, 'leaf'), as said below
- leaf_live: int32 [128], P('leaf'), may hold values from 1 to 4
- targets: int32 [7, 128], replicated, may hold values from 0 to 127, as said below
Outputs:
- leaf_solution: float32 [2, 64, 65536], P(None, 'rhs', 'leaf')
- sep_solution: float32 [2, 64, 7, 1024], P(None, 'rhs', None, 'leaf')
The draws below stay inside these ranges and needn't reach their ends.
Inputs may be any that keep to these rules, and one draw needn't show every extreme that they name: `targets`: in row l, the entries of each aligned group of 2 ** (l + 1) devices are a permutation of 0 to 2 ** (l + 1) - 1. Rows of a leaf front beyond 128 * leaf_live are padding and are ignored. `sep_inv`: entries are independent, of mean zero, with spread inversely proportional to the square root of the front's order. `sep_low`: entries are independent, of mean zero, with spread inversely proportional to the square root of the front's order.
All inputs are finite; a program needn't handle non-finite values.
Results may differ from the reference program's by a relative error of at most 0.025.
Values may be sent and summed in bfloat16 or wider, within the bound.
A program may use at most 64 MiB of HBM per device.

```python
import jax
import jax.numpy as jnp
from jax import lax

PR = 8
LEAF = 512
NRHS = 64
LEVELS = 7
N_LEAF = 128


def front_order(column, depth):
    block_step = column // PR + 2
    front_size = jnp.ones_like(block_step)
    for exponent in range(1, depth + 1):
        front_size = jnp.where(block_step >= 2 ** exponent, 2 ** exponent, front_size)
    return front_size


def scaled_factor(key, slab):
    column = jnp.arange(N_LEAF * slab, dtype=jnp.int32) % slab
    front_size = front_order(column, LEVELS).astype(jnp.float32)
    spread_scale = 1.0 / jnp.sqrt(2.0 * PR * front_size)
    values = jax.random.normal(key, (2, PR, N_LEAF * slab), jnp.float32)
    return (values * spread_scale[None, None, :]).astype(jnp.bfloat16)


def draw_sep_inv(key, part):
    return scaled_factor(jax.random.fold_in(key, 11), PR * (2 * N_LEAF - 2))


def draw_sep_low(key, part):
    return scaled_factor(jax.random.fold_in(key, 23), PR * (N_LEAF - 2))


def draw_targets(key, part):
    rows_list = []
    for level_now in range(LEVELS):
        group_size = 2 ** (level_now + 1)
        keys_list = jax.random.split(jax.random.fold_in(key, level_now + 37), N_LEAF // group_size)
        shuffled = jax.vmap(lambda one_key: jax.random.permutation(one_key, group_size))(keys_list)
        rows_list.append(shuffled.reshape(N_LEAF).astype(jnp.int32))
    return jnp.stack(rows_list)


def with_ends(values, own_key, low, high):
    spot = [jax.random.randint(jax.random.fold_in(own_key, axis), (), 0, length) for axis, length in enumerate(values.shape)]
    longest = values.shape.index(max(values.shape))
    neighbour = spot[:longest] + [(spot[longest] + 1) % values.shape[longest]] + spot[longest + 1:]
    return values.at[tuple(spot)].set(low).at[tuple(neighbour)].set(high)


def levels(own_key, dims, cuts, least, largest):
    def one(position, shards_of):
        heights = jax.random.uniform(jax.random.fold_in(jax.random.fold_in(own_key, 6), position), (shards_of,), jnp.float32, least / len(cuts), largest / len(cuts))
        return jnp.repeat(jnp.exp(heights), dims[position] // shards_of).reshape((-1,) + (1,) * (len(dims) - position - 1))

    level = one(*cuts[0])
    for cut in cuts[1:]:
        level = level * one(*cut)
    return level


def centred(own_key, shape, spread, most, cuts=(), kind=jnp.bfloat16):
    values = jax.random.normal(own_key, shape, jnp.float32) * spread
    if len(cuts) > 0:
        values = levels(own_key, shape, cuts, -0.22, 0.18) * values
    return jnp.clip(values, min=-most, max=most).astype(kind)


def setup_inputs(seed: int = 0) -> dict:
    key_of = jax.random.split(jax.random.key(seed), 9)
    leaf_rhs = centred(key_of[0], (2, NRHS, N_LEAF * LEAF), 1.0, 6.0, ((1, 4), (2, 128)), jnp.float32)
    sep_rhs = centred(key_of[1], (2, NRHS, LEVELS, N_LEAF * PR), 1.0, 6.0, ((1, 4), (3, 128)), jnp.float32)
    leaf_inv = centred(key_of[2], (2, LEAF, N_LEAF * LEAF), (2 * LEAF) ** -0.5, 0.1875, ((1, 4), (2, 128)))
    leaf_low = centred(key_of[3], (2, LEAF, N_LEAF * PR), (2 * LEAF) ** -0.5, 0.1875, ((2, 128),))
    sep_inv = draw_sep_inv(jax.random.fold_in(key_of[8], 71), 0)
    sep_low = draw_sep_low(jax.random.fold_in(key_of[8], 71), 0)
    leaf_live = with_ends(jax.random.randint(key_of[6], (N_LEAF,), 1, LEAF // 128 + 1), jax.random.fold_in(key_of[6], 1), 1, (LEAF // 128 + 1) - 1).astype(jnp.int32)
    targets = draw_targets(jax.random.fold_in(key_of[8], 71), 0)
    return dict(leaf_rhs=leaf_rhs, sep_rhs=sep_rhs, leaf_inv=leaf_inv, leaf_low=leaf_low, sep_inv=sep_inv, sep_low=sep_low, leaf_live=leaf_live, targets=targets)


exact_mode = lax.Precision.HIGHEST


def complex_product(operand, factor, form):
    operand = operand.astype(jnp.float32)
    factor = factor.astype(jnp.float32)
    real_part = jnp.einsum(form, operand[0], factor[0], precision=exact_mode) - jnp.einsum(form, operand[1], factor[1], precision=exact_mode)
    imag_part = jnp.einsum(form, operand[0], factor[1], precision=exact_mode) + jnp.einsum(form, operand[1], factor[0], precision=exact_mode)
    return jnp.stack([real_part, imag_part])


def destination(targets, level_now):
    group_size = 2 ** (level_now + 1)
    source = jnp.arange(N_LEAF, dtype=jnp.int32)
    target_block = (source // group_size) * group_size + targets[level_now].astype(jnp.int32)
    return (target_block[:, None] == source[None, :]).astype(jnp.float32)


def rounded(values_in):
    return lax.optimization_barrier(values_in.astype(jnp.bfloat16)).astype(jnp.float32)


def reference(leaf_rhs, sep_rhs, leaf_inv, leaf_low, sep_inv, sep_low, leaf_live, targets):
    slab_inv = PR * (2 * N_LEAF - 2)
    slab_low = PR * (N_LEAF - 2)
    live_mask = (jnp.arange(LEAF)[None, :] < leaf_live[:, None] * 128).astype(jnp.float32)
    leaf_z = (leaf_rhs.reshape(2, NRHS, N_LEAF, LEAF) * live_mask[None, None]).astype(jnp.bfloat16)
    leaf_factor = leaf_inv.reshape(2, LEAF, N_LEAF, LEAF)
    leaf_panel = leaf_low.reshape(2, LEAF, N_LEAF, PR)
    leaf_w = complex_product(leaf_z, leaf_factor, 'rdi,idj->rdj') * live_mask[None, None]
    update = complex_product(leaf_z, leaf_panel, 'rdi,idp->rdp')
    inv_all = sep_inv.reshape(2, PR, N_LEAF, slab_inv)
    low_all = sep_low.reshape(2, PR, N_LEAF, slab_low)
    solved_w = []
    panels = []
    for level_now in range(1, LEVELS + 1):
        group_size = 2 ** level_now
        fronts = N_LEAF // group_size
        offset = PR * (group_size - 2)
        arriving = jnp.einsum('crjp,jn->crnp', update, destination(targets, level_now - 1), precision=exact_mode)
        level_z = (sep_rhs[:, :, level_now - 1].reshape(2, NRHS, N_LEAF, PR) - arriving).astype(jnp.bfloat16)
        front_z = level_z.reshape(2, NRHS, fronts, group_size, PR)
        inv_front = inv_all[..., offset: offset + PR * group_size].reshape(2, PR, fronts, group_size, PR * group_size)
        solved_w.append(complex_product(front_z, inv_front, 'rfmi,ifmj->rfj').reshape(2, NRHS, N_LEAF, PR))
        if level_now < LEVELS:
            low_front = low_all[..., offset: offset + PR * group_size].reshape(2, PR, fronts, group_size, PR * group_size)
            panels.append(low_front)
            update = complex_product(front_z, low_front, 'rfmi,ifmj->rfj').reshape(2, NRHS, N_LEAF, PR)
    solved_x = [solved_w[level_now] for level_now in range(LEVELS)]
    for level_now in range(LEVELS - 1, 0, -1):
        group_size = 2 ** level_now
        fronts = N_LEAF // group_size
        parent_x = rounded(solved_x[level_now])
        gathered = jnp.einsum('crnp,jn->crjp', parent_x, destination(targets, level_now), precision=exact_mode)
        front_g = gathered.reshape(2, NRHS, fronts, group_size * PR)
        solved_x[level_now - 1] = solved_w[level_now - 1] - complex_product(front_g, panels[level_now - 1], 'rfj,ifmj->rfmi').reshape(2, NRHS, N_LEAF, PR)
    parent_x = rounded(solved_x[0])
    gathered = jnp.einsum('crnp,jn->crjp', parent_x, destination(targets, 0), precision=exact_mode)
    leaf_x = (leaf_w - complex_product(gathered, leaf_panel, 'rdp,idp->rdi')) * live_mask[None, None]
    return leaf_x.reshape(2, NRHS, N_LEAF * LEAF), jnp.stack(solved_x, axis=2).reshape(2, NRHS, LEVELS, N_LEAF * PR)
```

```python
import jax
import jax.numpy as jnp
from jax import lax
from jax.experimental import pallas as pl
from jax.experimental.pallas import tpu as pltpu
from jax.sharding import PartitionSpec as P

MESH = pl.DeviceIdType.MESH
bf16 = jnp.bfloat16
f32 = jnp.float32

COUNTS = dict(
    msg=15, zx=3, c0=7, c1=7, c2=7, c3=7, c4=7, t0=1, t1=1, t2=1, t3=1, t4=1,
    u4=1, u5=3, u6=7, w7=7, x7=7, x6=3, x5=1, w5=1, w6=3, lw=3,
)
FIRST = {}
_total = 0
for _name, _count in COUNTS.items():
    FIRST[_name] = _total
    _total += _count
COPIES = _total


def mm(a, b):
    return jnp.dot(a, b, preferred_element_type=f32)


def mm_nt(a, b):
    return lax.dot_general(a, b, (((1,), (1,)), ((), ())), preferred_element_type=f32)


def flip(value, mask):
    out = value
    for bit in range(3):
        if mask >> bit & 1:
            here = lax.rem(lax.div(value, 1 << bit), 2)
            out = out + (1 - 2 * here) * (1 << bit)
    return out


def iota(shape, axis):
    return lax.broadcasted_iota(jnp.int32, shape, axis)


def kernel(
    rhs_ref, sep_ref, inv_ref, low_ref, sinv_ref, slow_ref, live_ref, tgt_ref,
    leaf_out, sep_out,
    st, pk, m0, c0, c1, c2, c3, c4, zxs, zxr, eh, tt, p0, pis, pi4, rs_, vs, bs,
    m123, m4, m5, m6, i14, i5, i6, i7,
    s4, r4, s5, r5, s6, r6, s7, r7, xb7, xb6, xb5, sw5, rw5, sw6, rw6, w5o, w6o,
    lws, lwr, lwo, xo, xt, ssem, rsem,
):
    leaf = lax.axis_index("leaf")
    x = lax.axis_index("rhs")
    c = lax.rem(leaf, 2)
    y = lax.rem(lax.div(leaf, 2), 8)
    z = lax.div(leaf, 16)
    dl = lax.rem(leaf, 16)

    def dev(zz, yy, cc, xx):
        return (zz * 16 + yy * 2 + cc, xx)

    layer = [(k >> 1, k & 1) for k in range(1, 16)]
    barrier = pltpu.get_barrier_semaphore()

    def greet(device):
        pl.semaphore_signal(barrier, inc=1, device_id=device, device_id_type=MESH)

    for ky, kc in layer:
        greet(dev(z, flip(y, ky), flip(c, kc), x))
    for k in range(1, 8):
        greet(dev(flip(z, k), y, c, x))
    for k in range(1, 4):
        greet(dev(z, y, c, flip(x, k)))

    pending = []

    def copy(name, j, src, dst, device):
        index = FIRST[name] + j
        return pltpu.make_async_remote_copy(
            src_ref=src, dst_ref=dst, send_sem=ssem.at[index], recv_sem=rsem.at[index],
            device_id=device, device_id_type=MESH,
        )

    def send(name, j, src, dst, device):
        out = copy(name, j, src, dst, device)
        out.start()
        pending.append(out)
        return out

    live = live_ref[0]
    mask = iota((1, 512), 1) < live * 128
    zr = jnp.where(mask, rhs_ref[0], 0.0).astype(bf16)
    zi = jnp.where(mask, rhs_ref[1], 0.0).astype(bf16)
    er = low_ref[0].astype(f32)
    ei = low_ref[1].astype(f32)
    ehv = jnp.concatenate(
        [jnp.concatenate([er, -ei], axis=1), jnp.concatenate([ei, er], axis=1)], axis=0
    ).astype(bf16)
    eh[...] = ehv
    zcat = jnp.concatenate([zr, zi], axis=1)
    st[:, 112:128] = mm_nt(ehv, zcat)
    for level in range(7):
        st[0:8, 16 * level : 16 * level + 16] = sep_ref[0, level]
        st[8:16, 16 * level : 16 * level + 16] = sep_ref[1, level]
    m0[y, c] = st[...].astype(bf16)
    for q in range(4):
        zxs[q, 0] = zr[:, 128 * q : 128 * q + 128]
        zxs[q, 1] = zi[:, 128 * q : 128 * q + 128]
    zxr[x] = zxs[x]
    pk[:, 0:128] = jnp.zeros((16, 128), f32)
    pk[:, 1024:1152] = jnp.zeros((16, 128), f32)
    for part in range(2):
        pk[8 * part : 8 * part + 8, 16:1024] = slow_ref[part].astype(f32)
        pk[8 * part : 8 * part + 8, 1040:3072] = sinv_ref[part].astype(f32)
    c0[y, c, :, 0:256] = pk[:, 0:256].astype(bf16)
    c0[y, c, :, 256:512] = pk[:, 1024:1280].astype(bf16)
    c1[y, c] = pk[:, 256:512].astype(bf16)
    c2[y, c] = pk[:, 512:1024].astype(bf16)
    c3[y, c] = pk[:, 2048:3072].astype(bf16)
    c4[y, c] = pk[:, 1280:2048].astype(bf16)

    pl.semaphore_wait(barrier, 25)

    got = {name: [] for name in COUNTS}
    for j, (ky, kc) in enumerate(layer):
        got["msg"].append(
            send("msg", j, m0.at[y, c], m0.at[y, c], dev(z, flip(y, ky), flip(c, kc), x))
        )
    chunks = [("c0", c0), ("c1", c1), ("c2", c2), ("c3", c3), ("c4", c4)]

    def scatter(name, buf):
        for k in range(1, 8):
            got[name].append(
                send(name, k - 1, buf.at[y, c], buf.at[y, c], dev(z, flip(y, k), c, x))
            )

    scatter("c0", c0)
    for k in range(1, 4):
        got["zx"].append(
            send("zx", k - 1, zxs.at[flip(x, k)], zxr.at[x], dev(z, y, c, flip(x, k)))
        )
    for name, buf in chunks[1:]:
        scatter(name, buf)

    def arrive(name):
        for one in got[name]:
            one.wait_recv()

    def twin(index):
        name, buf = chunks[index]
        arrive(name)
        got["t%d" % index].append(
            send("t%d" % index, 0, buf.at[:, c], buf.at[:, c], dev(z, y, 1 - c, x))
        )

    tgt = tgt_ref[...].astype(f32).astype(bf16)
    row = iota((256, 128), 0)
    col = iota((256, 128), 1)
    quad = lax.div(z, 4) * 4
    for s in range(4):
        pick = col == (quad + s) * 16 + (row % 128) // 8
        tt[s] = mm_nt(pick.astype(f32).astype(bf16), tgt)
    pick = col == z * 16 + row // 16
    own0 = mm_nt(pick.astype(f32).astype(bf16), tgt)
    lane = iota((256, 256), 1).astype(f32)
    rown = iota((256, 1), 0)
    inner = (rown // 128 * 8 + rown % 8).astype(f32)
    p0[...] = (
        lane == (rown // 32 * 32 + rown % 16).astype(f32) + 16.0 * own0[:, 0:1]
    ).astype(f32).astype(bf16)
    zq = lax.rem(z, 4)
    zp = lax.rem(z, 2)
    mine = tt[zq]
    for level in range(1, 4):
        base = (rown % 128 // 8 // (2 << level) * (2 << level) * 16).astype(f32) + inner
        pis[level - 1] = (lane == base + 16.0 * mine[:, level : level + 1]).astype(f32).astype(bf16)
    for t in range(2):
        pi4[t] = (
            lane + 256.0 * t == inner + 16.0 * mine[:, 4:5]
        ).astype(f32).astype(bf16)
    natural = (lane == (rown % 128 // 8 * 16).astype(f32) + inner).astype(f32).astype(bf16)
    sign_row = (1 - 2 * (iota((256, 1), 0) // 8 % 2)).astype(f32)
    sign_lane = (1 - 2 * (iota((1, 256), 1) // 8 % 2)).astype(f32)

    def embed(raw):
        parts = raw.reshape(16, 2, 8, 128)
        swapped = jnp.concatenate([parts[:, 1:2], parts[:, 0:1]], axis=1).reshape(256, 128)
        return jnp.concatenate([raw * sign_row, swapped], axis=1).astype(bf16)

    def small(raw, level):
        size = 8 << level
        at = iota((128, 128), 0)
        to = iota((128, 128), 1)
        repeat = (at == size + to % size).astype(f32).astype(bf16)
        wide = mm(raw, repeat)
        front = iota((256, 128), 0) // (16 << level) == iota((256, 128), 1) // size
        return embed(jnp.where(front, wide, 0.0))

    arrive("msg")
    flipped = jnp.transpose(m0[...].reshape(256, 128).astype(f32))
    rs_[...] = flipped
    u = mm(flipped[112:128].astype(bf16), p0[...])
    twin(0)
    v = (flipped[0:16] - u).astype(bf16)
    vs[0] = v
    arrive("t0")
    raw0 = c0[:, :, :, 0:128].reshape(256, 128)
    for level in range(1, 4):
        m123[level - 1] = mm(small(raw0, level), pis[level - 1]).astype(bf16)
        u = mm(v, m123[level - 1])
        v = (rs_[16 * level : 16 * level + 16] - u).astype(bf16)
        vs[level] = v
    b4 = embed(c0[:, :, :, 128:256].reshape(256, 128).astype(f32))
    for t in range(2):
        m4[t] = mm(b4, pi4[t]).astype(bf16)
    s4[...] = mm(v, m4[1 - zp]).astype(bf16)
    got["u4"].append(send("u4", 0, s4, r4, dev(flip(z, 1), y, c, x)))
    u = mm(v, m4[zp])

    twin(1)
    arrive("t1")
    pair = lax.div(zq, 2) * 2
    for s in range(2):
        bs[s] = embed(c1[:, :, :, 128 * s : 128 * s + 128].reshape(256, 128).astype(f32))

    def fold5(t, carry):
        shift = (256 * t).astype(f32)
        total = jnp.zeros((256, 256), f32)
        for s in range(2):
            hot = lane + shift == inner + 16.0 * tt[pair + s][:, 5:6]
            total = total + mm(bs[s], hot.astype(f32).astype(bf16))
        m5[t] = total.astype(bf16)
        return carry

    lax.fori_loop(0, 4, fold5, 0)
    arrive("u4")
    v = (rs_[64:80] - u - r4[...].astype(f32)).astype(bf16)
    vs[4] = v
    for k in range(1, 4):
        s5[k - 1] = mm(v, m5[flip(zq, k)]).astype(bf16)
        got["u5"].append(send("u5", k - 1, s5.at[k - 1], r5.at[k - 1], dev(flip(z, k), y, c, x)))
    u = mm(v, m5[zq])

    twin(2)
    arrive("t2")
    for s in range(4):
        bs[s] = embed(c2[:, :, :, 128 * s : 128 * s + 128].reshape(256, 128).astype(f32))

    def fold6(t, carry):
        shift = (256 * t).astype(f32)
        total = jnp.zeros((256, 256), f32)
        for s in range(4):
            hot = lane + shift == inner + 16.0 * tt[s][:, 6:7]
            total = total + mm(bs[s], hot.astype(f32).astype(bf16))
        m6[t] = total.astype(bf16)
        return carry

    lax.fori_loop(0, 8, fold6, 0)
    arrive("u5")
    v = rs_[80:96] - u
    for k in range(3):
        v = v - r5[k].astype(f32)
    v = v.astype(bf16)
    vs[5] = v
    for k in range(1, 8):
        s6[k - 1] = mm(v, m6[flip(z, k)]).astype(bf16)
        got["u6"].append(send("u6", k - 1, s6.at[k - 1], r6.at[k - 1], dev(flip(z, k), y, c, x)))
    u = mm(v, m6[z])

    twin(3)
    arrive("t3")
    for s in range(8):
        i7[s] = mm(
            embed(c3[:, :, :, 128 * s : 128 * s + 128].reshape(256, 128).astype(f32)), natural
        ).astype(bf16)
    arrive("u6")
    v = rs_[96:112] - u
    for k in range(7):
        v = v - r6[k].astype(f32)
    v = v.astype(bf16)
    for k in range(1, 8):
        s7[k - 1] = mm(v, i7[flip(z, k)]).astype(bf16)
        got["w7"].append(send("w7", k - 1, s7.at[k - 1], r7.at[k - 1], dev(flip(z, k), y, c, x)))
    top = mm(v, i7[z])

    twin(4)
    arrive("t4")
    for s in range(2):
        i5[s] = mm(
            embed(c4[:, :, :, 128 * s : 128 * s + 128].reshape(256, 128).astype(f32)), natural
        ).astype(bf16)
    for s in range(4):
        i6[s] = mm(
            embed(c4[:, :, :, 256 + 128 * s : 384 + 128 * s].reshape(256, 128).astype(f32)), natural
        ).astype(bf16)
    sw5[...] = mm(vs[4], i5[1 - zp]).astype(bf16)
    got["w5"].append(send("w5", 0, sw5, rw5, dev(flip(z, 1), y, c, x)))
    for k in range(1, 4):
        sw6[k - 1] = mm(vs[5], i6[flip(zq, k)]).astype(bf16)
        got["w6"].append(send("w6", k - 1, sw6.at[k - 1], rw6.at[k - 1], dev(flip(z, k), y, c, x)))
    w5o[...] = mm(vs[4], i5[zp])
    w6o[...] = mm(vs[5], i6[zq])

    arrive("w7")
    for k in range(7):
        top = top + r7[k].astype(f32)
    top = top * sign_lane
    xo[96:112] = top
    xb7[z] = top.astype(bf16)
    for k in range(1, 8):
        got["x7"].append(send("x7", k - 1, xb7.at[z], xb7.at[z], dev(flip(z, k), y, c, x)))

    arrive("zx")
    zr4 = zxr[:, 0].reshape(64, 128)
    zi4 = zxr[:, 1].reshape(64, 128)
    panel = inv_ref[...].reshape(256, 512)
    real = mm(jnp.concatenate([zr4, -zi4], axis=1), panel).reshape(4, 16, 512)
    imag = mm(jnp.concatenate([zi4, zr4], axis=1), panel).reshape(4, 16, 512)
    lwo[:, 0] = real
    lwo[:, 1] = imag
    lws[:, 0] = real.astype(bf16)
    lws[:, 1] = imag.astype(bf16)
    for k in range(1, 4):
        got["lw"].append(
            send("lw", k - 1, lws.at[flip(x, k)], lwr.at[k - 1], dev(z, y, c, flip(x, k)))
        )

    rawi = c0[:, :, :, 256:384].reshape(256, 128)
    for level in range(1, 4):
        i14[level - 1] = mm(small(rawi, level), natural).astype(bf16)
    i14[3] = mm(embed(c0[:, :, :, 384:512].reshape(256, 128).astype(f32)), natural).astype(bf16)
    for level in range(1, 5):
        xo[16 * level - 16 : 16 * level] = mm(vs[level - 1], i14[level - 1]) * sign_lane
    arrive("w5")
    arrive("w6")
    xo[64:80] = (w5o[...] + rw5[...].astype(f32)) * sign_lane
    w6 = w6o[...]
    for k in range(3):
        w6 = w6 + rw6[k].astype(f32)
    w6 = w6 * sign_lane

    arrive("x7")
    for t in range(8):
        w6 = w6 - mm_nt(xb7[t], m6[t])
    xo[80:96] = w6
    xb6[zq] = w6.astype(bf16)
    for k in range(1, 4):
        got["x6"].append(send("x6", k - 1, xb6.at[zq], xb6.at[zq], dev(flip(z, k), y, c, x)))
    arrive("x6")
    w5 = xo[64:80]
    for t in range(4):
        w5 = w5 - mm_nt(xb6[t], m5[t])
    xo[64:80] = w5
    xb5[zp] = w5.astype(bf16)
    got["x5"].append(send("x5", 0, xb5.at[zp], xb5.at[zp], dev(flip(z, 1), y, c, x)))
    arrive("x5")
    now = xo[48:64]
    for t in range(2):
        now = now - mm_nt(xb5[t], m4[t])
    xo[48:64] = now
    for level in range(3, 0, -1):
        now = xo[16 * level - 16 : 16 * level] - mm_nt(now.astype(bf16), m123[level - 1])
        xo[16 * level - 16 : 16 * level] = now
    start = pl.multiple_of(dl * 16, 16)
    back = mm_nt(now.astype(bf16), p0[pl.ds(start, 16), :]).astype(bf16)
    less = mm(back, eh[...])
    arrive("lw")
    own = lwo[x]
    for k in range(3):
        own = own + lwr[k].astype(f32)
    leaf_out[0] = jnp.where(mask, own[0] - less[:, 0:512], 0.0)
    leaf_out[1] = jnp.where(mask, own[1] + less[:, 512:1024], 0.0)
    xo[112:128] = jnp.zeros((16, 256), f32)
    xt[...] = jnp.transpose(xo[...])
    mineT = xt[pl.ds(start, 16), :]
    for level in range(7):
        sep_out[0, level] = mineT[0:8, 16 * level : 16 * level + 16]
        sep_out[1, level] = -mineT[8:16, 16 * level : 16 * level + 16]

    for one in pending:
        one.wait_send()


def body(leaf_rhs, sep_rhs, leaf_inv, leaf_low, sep_inv, sep_low, leaf_live, targets):
    vm = pl.BlockSpec(memory_space=pltpu.VMEM)
    sm = pl.BlockSpec(memory_space=pltpu.SMEM)
    V = pltpu.VMEM
    out_leaf, out_sep = pl.pallas_call(
        kernel,
        out_shape=(
            jax.ShapeDtypeStruct((2, 16, 512), f32),
            jax.ShapeDtypeStruct((2, 7, 8, 16), f32),
        ),
        in_specs=[vm, vm, vm, vm, vm, vm, sm, vm],
        out_specs=(vm, vm),
        scratch_shapes=[
            V((16, 128), f32), V((16, 3072), f32), V((8, 2, 16, 128), bf16),
            V((8, 2, 16, 512), bf16), V((8, 2, 16, 256), bf16), V((8, 2, 16, 512), bf16),
            V((8, 2, 16, 1024), bf16), V((8, 2, 16, 768), bf16),
            V((4, 2, 16, 128), bf16), V((4, 2, 16, 128), bf16), V((16, 1024), bf16),
            V((4, 256, 7), f32), V((256, 256), bf16), V((3, 256, 256), bf16),
            V((2, 256, 256), bf16), V((128, 256), f32), V((6, 16, 256), bf16),
            V((4, 256, 256), bf16),
            V((3, 256, 256), bf16), V((2, 256, 256), bf16), V((4, 256, 256), bf16),
            V((8, 256, 256), bf16), V((4, 256, 256), bf16), V((2, 256, 256), bf16),
            V((4, 256, 256), bf16), V((8, 256, 256), bf16),
            V((16, 256), bf16), V((16, 256), bf16), V((3, 16, 256), bf16), V((3, 16, 256), bf16),
            V((7, 16, 256), bf16), V((7, 16, 256), bf16), V((7, 16, 256), bf16),
            V((7, 16, 256), bf16), V((8, 16, 256), bf16), V((4, 16, 256), bf16),
            V((2, 16, 256), bf16), V((16, 256), bf16), V((16, 256), bf16),
            V((3, 16, 256), bf16), V((3, 16, 256), bf16), V((16, 256), f32), V((16, 256), f32),
            V((4, 2, 16, 512), bf16), V((3, 2, 16, 512), bf16), V((4, 2, 16, 512), f32),
            V((128, 256), f32), V((256, 128), f32),
            pltpu.SemaphoreType.DMA((COPIES,)), pltpu.SemaphoreType.DMA((COPIES,)),
        ],
        compiler_params=pltpu.CompilerParams(
            collective_id=0, has_side_effects=True, vmem_limit_bytes=40 * 2**20
        ),
    )(
        leaf_rhs, sep_rhs.transpose(0, 2, 3, 1), leaf_inv, leaf_low.transpose(0, 2, 1),
        sep_inv, sep_low, leaf_live, targets,
    )
    return out_leaf, out_sep.transpose(0, 3, 1, 2)


def solution(mesh):
    placed = (
        P(None, "rhs", "leaf"),
        P(None, "rhs", None, "leaf"),
        P(None, "rhs", "leaf"),
        P(None, None, "leaf"),
        P(None, None, "leaf"),
        P(None, None, "leaf"),
        P("leaf"),
        P(),
    )
    return jax.shard_map(
        body,
        mesh=mesh,
        in_specs=placed,
        out_specs=(P(None, "rhs", "leaf"), P(None, "rhs", None, "leaf")),
        check_vma=False,
    )
```

```python
import jax
import jax.numpy as jnp
from jax import lax
from jax.experimental import pallas as pl
from jax.experimental.pallas import tpu as pltpu
from jax.sharding import PartitionSpec as P

MESH = pl.DeviceIdType.MESH
bf16 = jnp.bfloat16
f32 = jnp.float32

COUNTS = dict(
    msg=15, zx=3, c0=7, c1=7, c2=7, c3=7, c4=7, t0=1, t1=1, t2=1, t3=1, t4=1,
    u4=1, u5=3, u6=7, w7=7, x7=7, x6=3, x5=1, w5=1, w6=3, lw=3,
)
FIRST = {}
_total = 0
for _name, _count in COUNTS.items():
    FIRST[_name] = _total
    _total += _count
COPIES = _total


def mm(a, b):
    return jnp.dot(a, b, preferred_element_type=f32)


def mm_nt(a, b):
    return lax.dot_general(a, b, (((1,), (1,)), ((), ())), preferred_element_type=f32)


def flip(value, mask):
    out = value
    for bit in range(3):
        if mask >> bit & 1:
            here = lax.rem(lax.div(value, 1 << bit), 2)
            out = out + (1 - 2 * here) * (1 << bit)
    return out


def iota(shape, axis):
    return lax.broadcasted_iota(jnp.int32, shape, axis)


def kernel(
    rhs_hbm, sep_hbm, inv_hbm, low_hbm, sinv_hbm, slow_hbm, tgt_hbm, live_ref,
    leaf_out, sep_out,
    rhs_ref, sep_ref, inv_ref, low_ref, sinv_ref, slow_ref, tgt_ref, lsem,
    st, pk, m0, c0, c1, c2, c3, c4, zxs, zxr, eh, tt, p0, pis, pi4, rs_, vs, bs,
    m123, m4, m5, m6, i14, i5, i6, i7,
    s4, r4, s5, r5, s6, r6, s7, r7, xb7, xb6, xb5, sw5, rw5, sw6, rw6, w5o, w6o,
    lws, lwr, lwo, xo, xt, ssem, rsem,
):
    loads = []
    for j, (src, dst) in enumerate((
        (rhs_hbm, rhs_ref), (low_hbm, low_ref), (sep_hbm, sep_ref), (slow_hbm, slow_ref),
        (sinv_hbm, sinv_ref), (tgt_hbm, tgt_ref), (inv_hbm, inv_ref),
    )):
        loads.append(pltpu.make_async_copy(src, dst, lsem.at[j]))
        loads[-1].start()
    leaf = lax.axis_index("leaf")
    x = lax.axis_index("rhs")
    c = lax.rem(leaf, 2)
    y = lax.rem(lax.div(leaf, 2), 8)
    z = lax.div(leaf, 16)
    dl = lax.rem(leaf, 16)

    def dev(zz, yy, cc, xx):
        return (zz * 16 + yy * 2 + cc, xx)

    layer = [(k >> 1, k & 1) for k in range(1, 16)]
    barrier = pltpu.get_barrier_semaphore()

    def greet(device):
        pl.semaphore_signal(barrier, inc=1, device_id=device, device_id_type=MESH)

    for ky, kc in layer:
        greet(dev(z, flip(y, ky), flip(c, kc), x))
    for k in range(1, 8):
        greet(dev(flip(z, k), y, c, x))
    for k in range(1, 4):
        greet(dev(z, y, c, flip(x, k)))

    pending = []

    def copy(name, j, src, dst, device):
        index = FIRST[name] + j
        return pltpu.make_async_remote_copy(
            src_ref=src, dst_ref=dst, send_sem=ssem.at[index], recv_sem=rsem.at[index],
            device_id=device, device_id_type=MESH,
        )

    def send(name, j, src, dst, device):
        out = copy(name, j, src, dst, device)
        out.start()
        pending.append(out)
        return out

    loads[0].wait()
    loads[1].wait()
    live = live_ref[0]
    mask = iota((1, 512), 1) < live * 128
    zr = jnp.where(mask, rhs_ref[0], 0.0).astype(bf16)
    zi = jnp.where(mask, rhs_ref[1], 0.0).astype(bf16)
    er = low_ref[0].astype(f32)
    ei = low_ref[1].astype(f32)
    ehv = jnp.concatenate(
        [jnp.concatenate([er, -ei], axis=1), jnp.concatenate([ei, er], axis=1)], axis=0
    ).astype(bf16)
    eh[...] = ehv
    zcat = jnp.concatenate([zr, zi], axis=1)
    st[:, 112:128] = mm_nt(ehv, zcat)
    loads[2].wait()
    for level in range(7):
        st[0:8, 16 * level : 16 * level + 16] = sep_ref[0, level]
        st[8:16, 16 * level : 16 * level + 16] = sep_ref[1, level]
    m0[y, c] = st[...].astype(bf16)
    for q in range(4):
        zxs[q, 0] = zr[:, 128 * q : 128 * q + 128]
        zxs[q, 1] = zi[:, 128 * q : 128 * q + 128]
    zxr[x] = zxs[x]
    pk[:, 0:128] = jnp.zeros((16, 128), f32)
    pk[:, 1024:1152] = jnp.zeros((16, 128), f32)
    loads[3].wait()
    loads[4].wait()
    for part in range(2):
        pk[8 * part : 8 * part + 8, 16:1024] = slow_ref[part].astype(f32)
        pk[8 * part : 8 * part + 8, 1040:3072] = sinv_ref[part].astype(f32)
    c0[y, c, :, 0:256] = pk[:, 0:256].astype(bf16)
    c0[y, c, :, 256:512] = pk[:, 1024:1280].astype(bf16)
    c1[y, c] = pk[:, 256:512].astype(bf16)
    c2[y, c] = pk[:, 512:1024].astype(bf16)
    c3[y, c] = pk[:, 2048:3072].astype(bf16)
    c4[y, c] = pk[:, 1280:2048].astype(bf16)

    pl.semaphore_wait(barrier, 25)

    got = {name: [] for name in COUNTS}
    for j, (ky, kc) in enumerate(layer):
        got["msg"].append(
            send("msg", j, m0.at[y, c], m0.at[y, c], dev(z, flip(y, ky), flip(c, kc), x))
        )
    chunks = [("c0", c0), ("c1", c1), ("c2", c2), ("c3", c3), ("c4", c4)]

    def scatter(name, buf):
        for k in range(1, 8):
            got[name].append(
                send(name, k - 1, buf.at[y, c], buf.at[y, c], dev(z, flip(y, k), c, x))
            )

    scatter("c0", c0)
    for k in range(1, 4):
        got["zx"].append(
            send("zx", k - 1, zxs.at[flip(x, k)], zxr.at[x], dev(z, y, c, flip(x, k)))
        )
    for name, buf in chunks[1:]:
        scatter(name, buf)

    def arrive(name):
        for one in got[name]:
            one.wait_recv()

    def twin(index):
        name, buf = chunks[index]
        arrive(name)
        got["t%d" % index].append(
            send("t%d" % index, 0, buf.at[:, c], buf.at[:, c], dev(z, y, 1 - c, x))
        )

    loads[5].wait()
    tgt = tgt_ref[...].astype(f32).astype(bf16)
    row = iota((256, 128), 0)
    col = iota((256, 128), 1)
    quad = lax.div(z, 4) * 4
    for s in range(4):
        pick = col == (quad + s) * 16 + (row % 128) // 8
        tt[s] = mm_nt(pick.astype(f32).astype(bf16), tgt)
    pick = col == z * 16 + row // 16
    own0 = mm_nt(pick.astype(f32).astype(bf16), tgt)
    lane = iota((256, 256), 1).astype(f32)
    rown = iota((256, 1), 0)
    inner = (rown // 128 * 8 + rown % 8).astype(f32)
    p0[...] = (
        lane == (rown // 32 * 32 + rown % 16).astype(f32) + 16.0 * own0[:, 0:1]
    ).astype(f32).astype(bf16)
    zq = lax.rem(z, 4)
    zp = lax.rem(z, 2)
    mine = tt[zq]
    for level in range(1, 4):
        base = (rown % 128 // 8 // (2 << level) * (2 << level) * 16).astype(f32) + inner
        pis[level - 1] = (lane == base + 16.0 * mine[:, level : level + 1]).astype(f32).astype(bf16)
    for t in range(2):
        pi4[t] = (
            lane + 256.0 * t == inner + 16.0 * mine[:, 4:5]
        ).astype(f32).astype(bf16)
    natural = (lane == (rown % 128 // 8 * 16).astype(f32) + inner).astype(f32).astype(bf16)
    sign_row = (1 - 2 * (iota((256, 1), 0) // 8 % 2)).astype(f32)
    sign_lane = (1 - 2 * (iota((1, 256), 1) // 8 % 2)).astype(f32)

    def embed(raw):
        parts = raw.reshape(16, 2, 8, 128)
        swapped = jnp.concatenate([parts[:, 1:2], parts[:, 0:1]], axis=1).reshape(256, 128)
        return jnp.concatenate([raw * sign_row, swapped], axis=1).astype(bf16)

    def small(raw, level):
        size = 8 << level
        at = iota((128, 128), 0)
        to = iota((128, 128), 1)
        repeat = (at == size + to % size).astype(f32).astype(bf16)
        wide = mm(raw, repeat)
        front = iota((256, 128), 0) // (16 << level) == iota((256, 128), 1) // size
        return embed(jnp.where(front, wide, 0.0))

    arrive("msg")
    flipped = jnp.transpose(m0[...].reshape(256, 128).astype(f32))
    rs_[...] = flipped
    u = mm(flipped[112:128].astype(bf16), p0[...])
    twin(0)
    v = (flipped[0:16] - u).astype(bf16)
    vs[0] = v
    arrive("t0")
    raw0 = c0[:, :, :, 0:128].reshape(256, 128)
    for level in range(1, 4):
        m123[level - 1] = mm(small(raw0, level), pis[level - 1]).astype(bf16)
        u = mm(v, m123[level - 1])
        v = (rs_[16 * level : 16 * level + 16] - u).astype(bf16)
        vs[level] = v
    b4 = embed(c0[:, :, :, 128:256].reshape(256, 128).astype(f32))
    for t in range(2):
        m4[t] = mm(b4, pi4[t]).astype(bf16)
    s4[...] = mm(v, m4[1 - zp]).astype(bf16)
    got["u4"].append(send("u4", 0, s4, r4, dev(flip(z, 1), y, c, x)))
    u = mm(v, m4[zp])

    twin(1)
    arrive("t1")
    pair = lax.div(zq, 2) * 2
    for s in range(2):
        bs[s] = embed(c1[:, :, :, 128 * s : 128 * s + 128].reshape(256, 128).astype(f32))

    def fold5(t, carry):
        shift = (256 * t).astype(f32)
        total = jnp.zeros((256, 256), f32)
        for s in range(2):
            hot = lane + shift == inner + 16.0 * tt[pair + s][:, 5:6]
            total = total + mm(bs[s], hot.astype(f32).astype(bf16))
        m5[t] = total.astype(bf16)
        return carry

    lax.fori_loop(0, 4, fold5, 0)
    arrive("u4")
    v = (rs_[64:80] - u - r4[...].astype(f32)).astype(bf16)
    vs[4] = v
    for k in range(1, 4):
        s5[k - 1] = mm(v, m5[flip(zq, k)]).astype(bf16)
        got["u5"].append(send("u5", k - 1, s5.at[k - 1], r5.at[k - 1], dev(flip(z, k), y, c, x)))
    u = mm(v, m5[zq])

    twin(2)
    arrive("t2")
    for s in range(4):
        bs[s] = embed(c2[:, :, :, 128 * s : 128 * s + 128].reshape(256, 128).astype(f32))

    def fold6(t, carry):
        shift = (256 * t).astype(f32)
        total = jnp.zeros((256, 256), f32)
        for s in range(4):
            hot = lane + shift == inner + 16.0 * tt[s][:, 6:7]
            total = total + mm(bs[s], hot.astype(f32).astype(bf16))
        m6[t] = total.astype(bf16)
        return carry

    lax.fori_loop(0, 8, fold6, 0)
    arrive("u5")
    v = rs_[80:96] - u
    for k in range(3):
        v = v - r5[k].astype(f32)
    v = v.astype(bf16)
    vs[5] = v
    for k in range(1, 8):
        s6[k - 1] = mm(v, m6[flip(z, k)]).astype(bf16)
        got["u6"].append(send("u6", k - 1, s6.at[k - 1], r6.at[k - 1], dev(flip(z, k), y, c, x)))
    u = mm(v, m6[z])

    twin(3)
    arrive("t3")
    for s in range(8):
        i7[s] = mm(
            embed(c3[:, :, :, 128 * s : 128 * s + 128].reshape(256, 128).astype(f32)), natural
        ).astype(bf16)
    arrive("u6")
    v = rs_[96:112] - u
    for k in range(7):
        v = v - r6[k].astype(f32)
    v = v.astype(bf16)
    for k in range(1, 8):
        s7[k - 1] = mm(v, i7[flip(z, k)]).astype(bf16)
        got["w7"].append(send("w7", k - 1, s7.at[k - 1], r7.at[k - 1], dev(flip(z, k), y, c, x)))
    top = mm(v, i7[z])

    twin(4)
    arrive("t4")
    for s in range(2):
        i5[s] = mm(
            embed(c4[:, :, :, 128 * s : 128 * s + 128].reshape(256, 128).astype(f32)), natural
        ).astype(bf16)
    for s in range(4):
        i6[s] = mm(
            embed(c4[:, :, :, 256 + 128 * s : 384 + 128 * s].reshape(256, 128).astype(f32)), natural
        ).astype(bf16)
    sw5[...] = mm(vs[4], i5[1 - zp]).astype(bf16)
    got["w5"].append(send("w5", 0, sw5, rw5, dev(flip(z, 1), y, c, x)))
    for k in range(1, 4):
        sw6[k - 1] = mm(vs[5], i6[flip(zq, k)]).astype(bf16)
        got["w6"].append(send("w6", k - 1, sw6.at[k - 1], rw6.at[k - 1], dev(flip(z, k), y, c, x)))
    w5o[...] = mm(vs[4], i5[zp])
    w6o[...] = mm(vs[5], i6[zq])

    arrive("w7")
    for k in range(7):
        top = top + r7[k].astype(f32)
    top = top * sign_lane
    xo[96:112] = top
    xb7[z] = top.astype(bf16)
    for k in range(1, 8):
        got["x7"].append(send("x7", k - 1, xb7.at[z], xb7.at[z], dev(flip(z, k), y, c, x)))

    arrive("zx")
    zr4 = zxr[:, 0].reshape(64, 128)
    zi4 = zxr[:, 1].reshape(64, 128)
    loads[6].wait()
    panel = inv_ref[...].reshape(256, 512)
    real = mm(jnp.concatenate([zr4, -zi4], axis=1), panel).reshape(4, 16, 512)
    imag = mm(jnp.concatenate([zi4, zr4], axis=1), panel).reshape(4, 16, 512)
    lwo[:, 0] = real
    lwo[:, 1] = imag
    lws[:, 0] = real.astype(bf16)
    lws[:, 1] = imag.astype(bf16)
    for k in range(1, 4):
        got["lw"].append(
            send("lw", k - 1, lws.at[flip(x, k)], lwr.at[k - 1], dev(z, y, c, flip(x, k)))
        )

    rawi = c0[:, :, :, 256:384].reshape(256, 128)
    for level in range(1, 4):
        i14[level - 1] = mm(small(rawi, level), natural).astype(bf16)
    i14[3] = mm(embed(c0[:, :, :, 384:512].reshape(256, 128).astype(f32)), natural).astype(bf16)
    for level in range(1, 5):
        xo[16 * level - 16 : 16 * level] = mm(vs[level - 1], i14[level - 1]) * sign_lane
    arrive("w5")
    arrive("w6")
    xo[64:80] = (w5o[...] + rw5[...].astype(f32)) * sign_lane
    w6 = w6o[...]
    for k in range(3):
        w6 = w6 + rw6[k].astype(f32)
    w6 = w6 * sign_lane

    arrive("x7")
    for t in range(8):
        w6 = w6 - mm_nt(xb7[t], m6[t])
    xo[80:96] = w6
    xb6[zq] = w6.astype(bf16)
    for k in range(1, 4):
        got["x6"].append(send("x6", k - 1, xb6.at[zq], xb6.at[zq], dev(flip(z, k), y, c, x)))
    arrive("x6")
    w5 = xo[64:80]
    for t in range(4):
        w5 = w5 - mm_nt(xb6[t], m5[t])
    xo[64:80] = w5
    xb5[zp] = w5.astype(bf16)
    got["x5"].append(send("x5", 0, xb5.at[zp], xb5.at[zp], dev(flip(z, 1), y, c, x)))
    arrive("x5")
    now = xo[48:64]
    for t in range(2):
        now = now - mm_nt(xb5[t], m4[t])
    xo[48:64] = now
    for level in range(3, 0, -1):
        now = xo[16 * level - 16 : 16 * level] - mm_nt(now.astype(bf16), m123[level - 1])
        xo[16 * level - 16 : 16 * level] = now
    start = pl.multiple_of(dl * 16, 16)
    back = mm_nt(now.astype(bf16), p0[pl.ds(start, 16), :]).astype(bf16)
    less = mm(back, eh[...])
    arrive("lw")
    own = lwo[x]
    for k in range(3):
        own = own + lwr[k].astype(f32)
    leaf_out[0] = jnp.where(mask, own[0] - less[:, 0:512], 0.0)
    leaf_out[1] = jnp.where(mask, own[1] + less[:, 512:1024], 0.0)
    xo[112:128] = jnp.zeros((16, 256), f32)
    xt[...] = jnp.transpose(xo[...])
    mineT = xt[pl.ds(start, 16), :]
    for level in range(7):
        sep_out[0, level] = mineT[0:8, 16 * level : 16 * level + 16]
        sep_out[1, level] = -mineT[8:16, 16 * level : 16 * level + 16]

    for one in pending:
        one.wait_send()


def body(leaf_rhs, sep_rhs, leaf_inv, leaf_low, sep_inv, sep_low, leaf_live, targets):
    vm = pl.BlockSpec(memory_space=pltpu.VMEM)
    hb = pl.BlockSpec(memory_space=pltpu.HBM)
    sm = pl.BlockSpec(memory_space=pltpu.SMEM)
    V = pltpu.VMEM
    out_leaf, out_sep = pl.pallas_call(
        kernel,
        out_shape=(
            jax.ShapeDtypeStruct((2, 16, 512), f32),
            jax.ShapeDtypeStruct((2, 7, 8, 16), f32),
        ),
        in_specs=[hb, hb, hb, hb, hb, hb, hb, sm],
        out_specs=(vm, vm),
        scratch_shapes=[
            V((2, 16, 512), f32), V((2, 7, 8, 16), f32), V((2, 128, 512), bf16),
            V((2, 8, 512), bf16), V((2, 8, 2032), bf16), V((2, 8, 1008), bf16),
            V((7, 128), jnp.int32), pltpu.SemaphoreType.DMA((7,)),
            V((16, 128), f32), V((16, 3072), f32), V((8, 2, 16, 128), bf16),
            V((8, 2, 16, 512), bf16), V((8, 2, 16, 256), bf16), V((8, 2, 16, 512), bf16),
            V((8, 2, 16, 1024), bf16), V((8, 2, 16, 768), bf16),
            V((4, 2, 16, 128), bf16), V((4, 2, 16, 128), bf16), V((16, 1024), bf16),
            V((4, 256, 7), f32), V((256, 256), bf16), V((3, 256, 256), bf16),
            V((2, 256, 256), bf16), V((128, 256), f32), V((6, 16, 256), bf16),
            V((4, 256, 256), bf16),
            V((3, 256, 256), bf16), V((2, 256, 256), bf16), V((4, 256, 256), bf16),
            V((8, 256, 256), bf16), V((4, 256, 256), bf16), V((2, 256, 256), bf16),
            V((4, 256, 256), bf16), V((8, 256, 256), bf16),
            V((16, 256), bf16), V((16, 256), bf16), V((3, 16, 256), bf16), V((3, 16, 256), bf16),
            V((7, 16, 256), bf16), V((7, 16, 256), bf16), V((7, 16, 256), bf16),
            V((7, 16, 256), bf16), V((8, 16, 256), bf16), V((4, 16, 256), bf16),
            V((2, 16, 256), bf16), V((16, 256), bf16), V((16, 256), bf16),
            V((3, 16, 256), bf16), V((3, 16, 256), bf16), V((16, 256), f32), V((16, 256), f32),
            V((4, 2, 16, 512), bf16), V((3, 2, 16, 512), bf16), V((4, 2, 16, 512), f32),
            V((128, 256), f32), V((256, 128), f32),
            pltpu.SemaphoreType.DMA((COPIES,)), pltpu.SemaphoreType.DMA((COPIES,)),
        ],
        compiler_params=pltpu.CompilerParams(
            collective_id=0, has_side_effects=True, vmem_limit_bytes=60 * 2**20
        ),
    )(
        leaf_rhs, sep_rhs.transpose(0, 2, 3, 1), leaf_inv, leaf_low.transpose(0, 2, 1),
        sep_inv, sep_low, targets, leaf_live,
    )
    return out_leaf, out_sep.transpose(0, 3, 1, 2)


def solution(mesh):
    placed = (
        P(None, "rhs", "leaf"),
        P(None, "rhs", None, "leaf"),
        P(None, "rhs", "leaf"),
        P(None, None, "leaf"),
        P(None, None, "leaf"),
        P(None, None, "leaf"),
        P("leaf"),
        P(),
    )
    return jax.shard_map(
        body,
        mesh=mesh,
        in_specs=placed,
        out_specs=(P(None, "rhs", "leaf"), P(None, "rhs", None, "leaf")),
        check_vma=False,
    )
```

```python
import jax
import jax.numpy as jnp
from jax import lax
from jax.experimental import pallas as pl
from jax.experimental.pallas import tpu as pltpu
from jax.sharding import PartitionSpec as P

MESH = pl.DeviceIdType.MESH
bf16 = jnp.bfloat16
f32 = jnp.float32

COUNTS = dict(
    msg=15, zx=3, c0=7, c4=7, q1=1, q2=3, q3=7, c1=7, c2=7, c3=7, t0=1, t1=1, t2=1, t3=1, t4=1,
    h5=1, h6=3, h7=7, u4=1, u5=3, u6=7, d6=3, d5=1, g6=7, g5=3, g4=1, lw=3,
)
FIRST = {}
_total = 0
for _name, _count in COUNTS.items():
    FIRST[_name] = _total
    _total += _count
COPIES = _total


def mm(a, b):
    return jnp.dot(a, b, preferred_element_type=f32)


def mm_nt(a, b):
    return lax.dot_general(a, b, (((1,), (1,)), ((), ())), preferred_element_type=f32)


def flip(value, mask):
    out = value
    for bit in range(3):
        if mask >> bit & 1:
            here = lax.rem(lax.div(value, 1 << bit), 2)
            out = out + (1 - 2 * here) * (1 << bit)
    return out


def iota(shape, axis):
    return lax.broadcasted_iota(jnp.int32, shape, axis)


def hot(test):
    return test.astype(f32).astype(bf16)


def kernel(
    rhs_hbm, sep_hbm, inv_hbm, low_hbm, sinv_hbm, slow_hbm, tgt_hbm, live_ref, tgs,
    leaf_out, sep_out,
    rhs_ref, sep_ref, inv_ref, low_ref, sinv_ref, slow_ref, tgt_ref, lsem,
    st, pk, m0, c0, c4, p1, p2, p3, c1, c2, c3, zxs, zxr, eh, dl_, p0, pis, rs_, vs,
    m123, b4, b5, b6, b7, n5, n6, n7, i14, i5, i6, h5, h6, h7, u4g, u5g, u6g,
    wq6, wq5, d6s, d6r, d5s, d5r, g6g, g5g, g4g, lws, lwr, lwo, xo, xt, ssem, rsem,
):
    loads = []
    for j, (src, dst) in enumerate((
        (rhs_hbm, rhs_ref), (low_hbm, low_ref), (sep_hbm, sep_ref), (slow_hbm, slow_ref),
        (sinv_hbm, sinv_ref), (tgt_hbm, tgt_ref), (inv_hbm, inv_ref),
    )):
        loads.append(pltpu.make_async_copy(src, dst, lsem.at[j]))
        loads[-1].start()
    leaf = lax.axis_index("leaf")
    x = lax.axis_index("rhs")
    c = lax.rem(leaf, 2)
    y = lax.rem(lax.div(leaf, 2), 8)
    z = lax.div(leaf, 16)
    dl = lax.rem(leaf, 16)
    zq = lax.rem(z, 4)
    zp = lax.rem(z, 2)
    quad = z - zq
    pair = z - zp

    def dev(zz, yy, cc, xx):
        return (zz * 16 + yy * 2 + cc, xx)

    layer = [(k >> 1, k & 1) for k in range(1, 16)]
    barrier = pltpu.get_barrier_semaphore()

    def greet(device):
        pl.semaphore_signal(barrier, inc=1, device_id=device, device_id_type=MESH)

    for ky, kc in layer:
        greet(dev(z, flip(y, ky), flip(c, kc), x))
    for k in range(1, 8):
        greet(dev(flip(z, k), y, c, x))
    for k in range(1, 4):
        greet(dev(z, y, c, flip(x, k)))

    pending = []
    got = {name: [] for name in COUNTS}

    def send(name, src, dst, device):
        index = FIRST[name] + len(got[name])
        out = pltpu.make_async_remote_copy(
            src_ref=src, dst_ref=dst, send_sem=ssem.at[index], recv_sem=rsem.at[index],
            device_id=device, device_id_type=MESH,
        )
        out.start()
        pending.append(out)
        got[name].append(out)

    def arrive(name):
        for one in got[name]:
            one.wait_recv()

    def scatter(name, buf):
        for k in range(1, 8):
            send(name, buf.at[y, c], buf.at[y, c], dev(z, flip(y, k), c, x))

    def twin(name, tag, buf):
        arrive(name)
        send(tag, buf.at[:, c], buf.at[:, c], dev(z, y, 1 - c, x))

    def along(name, count, buf, slot):
        for k in range(1, count):
            send(name, buf.at[slot], buf.at[slot], dev(flip(z, k), y, c, x))

    loads[0].wait()
    loads[1].wait()
    live = live_ref[0]
    mask = iota((1, 512), 1) < live * 128
    zr = jnp.where(mask, rhs_ref[0], 0.0).astype(bf16)
    zi = jnp.where(mask, rhs_ref[1], 0.0).astype(bf16)
    er = low_ref[0].astype(f32)
    ei = low_ref[1].astype(f32)
    ehv = jnp.concatenate(
        [jnp.concatenate([er, -ei], axis=1), jnp.concatenate([ei, er], axis=1)], axis=0
    ).astype(bf16)
    eh[...] = ehv
    zcat = jnp.concatenate([zr, zi], axis=1)
    st[:, 112:128] = mm_nt(ehv, zcat)
    loads[2].wait()
    for level in range(7):
        st[0:8, 16 * level : 16 * level + 16] = sep_ref[0, level]
        st[8:16, 16 * level : 16 * level + 16] = sep_ref[1, level]
    m0[y, c] = st[...].astype(bf16)
    pk[:, 0:128] = jnp.zeros((16, 128), f32)
    pk[:, 1024:1152] = jnp.zeros((16, 128), f32)
    loads[3].wait()
    loads[4].wait()
    for part in range(2):
        pk[8 * part : 8 * part + 8, 16:1024] = slow_ref[part].astype(f32)
        pk[8 * part : 8 * part + 8, 1040:3072] = sinv_ref[part].astype(f32)
    c0[y, c, :, 0:256] = pk[:, 0:256].astype(bf16)
    c0[y, c, :, 256:512] = pk[:, 1024:1280].astype(bf16)
    c4[y, c] = pk[:, 1280:2048].astype(bf16)
    for q in range(4):
        zxs[q, 0] = zr[:, 128 * q : 128 * q + 128]
        zxs[q, 1] = zi[:, 128 * q : 128 * q + 128]
    zxr[x] = zxs[x]
    for t in range(2):
        p1[t] = pk[:, 256 + 128 * t : 384 + 128 * t].astype(bf16)
    for t in range(4):
        p2[t] = pk[:, 512 + 128 * t : 640 + 128 * t].astype(bf16)
    c1[y, c, zp] = p1[zp]
    c2[y, c, zq] = p2[zq]
    loads[5].wait()
    tgt = tgt_ref[...].astype(f32).astype(bf16)
    spot = iota((128, 1024), 1)
    wide = mm(tgt, hot(iota((128, 1024), 0) == spot // 8))
    place = 8.0 * wide[6:7] + (iota((1, 1024), 1) % 8).astype(f32)
    top_rows = pk[:, 2048:3072].astype(bf16)
    down = iota((1024, 256), 0).astype(f32)
    for t in range(4):
        moved = mm(top_rows, hot(down == place[:, 256 * t : 256 * t + 256])).astype(bf16)
        p3[2 * t] = moved[:, 0:128]
        p3[2 * t + 1] = moved[:, 128:256]
    c3[y, c, z] = p3[z]

    pl.semaphore_wait(barrier, 25)

    for ky, kc in layer:
        send("msg", m0.at[y, c], m0.at[y, c], dev(z, flip(y, ky), flip(c, kc), x))
    scatter("c0", c0)
    send("q1", p1.at[1 - zp], c1.at[y, c, zp], dev(flip(z, 1), y, c, x))
    for k in range(1, 4):
        send("q2", p2.at[flip(zq, k)], c2.at[y, c, zq], dev(flip(z, k), y, c, x))
    for k in range(1, 8):
        send("q3", p3.at[flip(z, k)], c3.at[y, c, z], dev(flip(z, k), y, c, x))
    for k in range(1, 4):
        send("zx", zxs.at[flip(x, k)], zxr.at[x], dev(z, y, c, flip(x, k)))

    lane16 = (iota((1, 256), 1) % 16).astype(f32)
    for s in range(8):
        pick = iota((128, 256), 0) == 16 * s + iota((128, 256), 1) // 16
        dl_[s, 0:7] = 16.0 * mm(tgt, hot(pick)) + lane16
    down = iota((256, 256), 0).astype(f32)

    def route(level, source, slab):
        shift = jnp.asarray(256 * slab, jnp.int32).astype(f32)
        return hot(down + shift == dl_[source][level : level + 1])

    p0[...] = hot(down == dl_[z][0:1] + (iota((1, 256), 1) // 32 * 32).astype(f32))
    lane = iota((1, 256), 1)
    pick = iota((128, 256), 0) == 16 * z + iota((128, 256), 1) % 128 // 8
    inner = (lane // 128 * 8 + lane % 8).astype(f32)
    old = 16.0 * mm(tgt, hot(pick)) + inner
    for level in range(1, 4):
        base = (lane % 128 // 8 // (2 << level) * (2 << level) * 16).astype(f32)
        pis[level - 1] = hot(down == old[level : level + 1] + base)
    rown = iota((256, 1), 0)
    natural = hot(iota((256, 256), 1) == rown % 128 // 8 * 16 + rown // 128 * 8 + rown % 8)
    sign_row = (1 - 2 * (iota((256, 1), 0) // 8 % 2)).astype(f32)
    sign_lane = (1 - 2 * (lane // 8 % 2)).astype(f32)

    def embed(raw):
        parts = raw.reshape(16, 2, 8, 128)
        swapped = jnp.concatenate([parts[:, 1:2], parts[:, 0:1]], axis=1).reshape(256, 128)
        return jnp.concatenate([raw * sign_row, swapped], axis=1).astype(bf16)

    def square(raw):
        return mm(embed(raw.reshape(256, 128).astype(f32)), natural).astype(bf16)

    def small(raw, level):
        size = 8 << level
        at = iota((128, 128), 0)
        to = iota((128, 128), 1)
        repeat = hot(at == size + to % size)
        spread = mm(raw, repeat)
        front = iota((256, 128), 0) // (16 << level) == iota((256, 128), 1) // size
        return embed(jnp.where(front, spread, 0.0))

    def blocks(ref, s):
        return ref[pl.ds(16 * s, 16)].reshape(256, 256)

    arrive("msg")
    flipped = jnp.transpose(m0[...].reshape(256, 128).astype(f32))
    rs_[...] = flipped
    u = mm_nt(flipped[112:128].astype(bf16), p0[...])
    v = (flipped[0:16] - u).astype(bf16)
    vs[0] = v
    twin("c0", "t0", c0)
    arrive("q1")
    scatter("c1", c1)
    arrive("q2")
    scatter("c2", c2)
    arrive("t0")
    raw0 = c0[:, :, :, 0:128].reshape(256, 128)
    for level in range(1, 4):
        m123[level - 1] = mm_nt(small(raw0, level), pis[level - 1]).astype(bf16)
        u = mm(v, m123[level - 1])
        v = (rs_[16 * level : 16 * level + 16] - u).astype(bf16)
        vs[level] = v
    b4[...] = square(c0[:, :, :, 128:256])
    own = mm(v, b4[...]).astype(bf16)
    u4g[zp] = own
    along("u4", 2, u4g, zp)
    h5[zp] = rs_[64:80].astype(bf16)
    h6[zq] = rs_[80:96].astype(bf16)
    h7[z] = rs_[96:112].astype(bf16)
    along("h5", 2, h5, zp)
    along("h6", 4, h6, zq)
    along("h7", 8, h7, z)
    arrive("q3")
    scatter("c3", c3)
    scatter("c4", c4)

    twin("c1", "t1", c1)
    arrive("t1")
    for s in range(2):
        b5[16 * s : 16 * s + 16] = square(c1[:, :, s]).reshape(16, 16, 256)

    def move(level, first, source, target):
        def step(i, carry):
            target[i] = source[tgs[level, first + i]]
            return carry
        return step

    lax.fori_loop(0, 32, move(4, 16 * pair, b5, n5), 0, unroll=8)
    arrive("h5")
    u = mm(h5[0], blocks(b5, 0)) + mm(h5[1], blocks(b5, 1)) - mm(own, blocks(n5, zp))
    arrive("u4")
    u = u - mm(u4g[1 - zp], blocks(n5, 1 - zp))
    own = u.astype(bf16)
    u5g[zq] = own
    along("u5", 4, u5g, zq)

    twin("c2", "t2", c2)
    arrive("t2")
    for s in range(4):
        b6[16 * s : 16 * s + 16] = square(c2[:, :, s]).reshape(16, 16, 256)
    lax.fori_loop(0, 64, move(5, 16 * quad, b6, n6), 0, unroll=8)
    arrive("h6")
    u = -mm(own, blocks(n6, zq))
    for s in range(4):
        u = u + mm(h6[s], blocks(b6, s))
    for k in range(1, 4):
        got["u5"][k - 1].wait_recv()
        u = u - mm(u5g[flip(zq, k)], blocks(n6, flip(zq, k)))
    own = u.astype(bf16)
    u6g[z] = own
    along("u6", 8, u6g, z)

    twin("c3", "t3", c3)
    arrive("t3")
    for s in range(8):
        b7[16 * s : 16 * s + 16] = square(c3[:, :, s]).reshape(16, 16, 256)
    lax.fori_loop(0, 128, move(6, 0, b7, n7), 0, unroll=8)
    arrive("h7")
    u = -mm(own, blocks(n7, z))
    for s in range(8):
        u = u + mm(h7[s], blocks(b7, s))

    twin("c4", "t4", c4)
    arrive("t4")
    v5 = rs_[64:80]
    for s in range(2):
        i5[s] = square(c4[:, :, :, 128 * s : 128 * s + 128])
        v5 = v5 - mm_nt(u4g[s], route(4, pair + s, zp))
    v5 = v5.astype(bf16)
    v6 = rs_[80:96]
    for s in range(4):
        i6[s] = square(c4[:, :, :, 256 + 128 * s : 384 + 128 * s])
        v6 = v6 - mm_nt(u5g[s], route(5, quad + s, zq))
    v6 = v6.astype(bf16)
    w6 = [mm(v6, i6[s]).astype(bf16) for s in range(4)]
    for s in range(4):
        total = mm(w6[0], route(5, quad + s, 0))
        for t in range(1, 4):
            total = total + mm(w6[t], route(5, quad + s, t))
        wq6[s] = total * sign_lane

    for k in range(1, 8):
        got["u6"][k - 1].wait_recv()
        u = u - mm(u6g[flip(z, k)], blocks(n7, flip(z, k)))
    own = (u * sign_lane).astype(bf16)

    for k in range(1, 4):
        t = flip(zq, k)
        d6s[k - 1] = (wq6[t] - mm_nt(own, blocks(n6, t))).astype(bf16)
        send("d6", d6s.at[k - 1], d6r.at[k - 1], dev(flip(z, k), y, c, x))
    below = wq6[zq] - mm_nt(own, blocks(n6, zq))
    g6g[z] = own
    along("g6", 8, g6g, z)

    w5 = [mm(v5, i5[s]).astype(bf16) for s in range(2)]
    for s in range(2):
        wq5[s] = sign_lane * (
            mm(w5[0], route(4, pair + s, 0)) + mm(w5[1], route(4, pair + s, 1))
        )
    arrive("d6")
    for k in range(3):
        below = below + d6r[k].astype(f32)
    own = below.astype(bf16)
    d5s[...] = (wq5[1 - zp] - mm_nt(own, blocks(n5, 1 - zp))).astype(bf16)
    send("d5", d5s, d5r, dev(flip(z, 1), y, c, x))
    below = wq5[zp] - mm_nt(own, blocks(n5, zp))
    g5g[zq] = own
    along("g5", 4, g5g, zq)

    arrive("zx")
    loads[6].wait()
    zr4 = zxr[:, 0].reshape(64, 128)
    zi4 = zxr[:, 1].reshape(64, 128)
    panel = inv_ref[...].reshape(256, 512)
    real = mm(jnp.concatenate([zr4, -zi4], axis=1), panel).reshape(4, 16, 512)
    imag = mm(jnp.concatenate([zi4, zr4], axis=1), panel).reshape(4, 16, 512)
    lwo[:, 0] = real
    lwo[:, 1] = imag
    lws[:, 0] = real.astype(bf16)
    lws[:, 1] = imag.astype(bf16)
    for k in range(1, 4):
        send("lw", lws.at[flip(x, k)], lwr.at[k - 1], dev(z, y, c, flip(x, k)))
    rawi = c0[:, :, :, 256:384].reshape(256, 128)
    for level in range(1, 4):
        i14[level - 1] = mm(small(rawi, level), natural).astype(bf16)
    i14[3] = square(c0[:, :, :, 384:512])
    for level in range(1, 5):
        xo[16 * level - 16 : 16 * level] = mm(vs[level - 1], i14[level - 1]) * sign_lane

    arrive("d5")
    own = (below + d5r[...].astype(f32)).astype(bf16)
    g4g[zp] = own
    along("g4", 2, g4g, zp)
    now = xo[48:64] - mm_nt(own, b4[...])
    xo[48:64] = now
    for level in range(3, 0, -1):
        now = xo[16 * level - 16 : 16 * level] - mm_nt(now.astype(bf16), m123[level - 1])
        xo[16 * level - 16 : 16 * level] = now
    parent = 16 * (dl - c + tgs[0, leaf])
    chosen = hot(iota((16, 256), 1) == parent + iota((16, 256), 0))
    back = mm_nt(now.astype(bf16), chosen).astype(bf16)
    less = mm(back, eh[...])
    arrive("lw")
    mine = lwo[x]
    for k in range(3):
        mine = mine + lwr[k].astype(f32)
    leaf_out[0] = jnp.where(mask, mine[0] - less[:, 0:512], 0.0)
    leaf_out[1] = jnp.where(mask, mine[1] + less[:, 512:1024], 0.0)

    xt[...] = jnp.transpose(xo[...])
    start = pl.multiple_of(dl * 16, 16)
    turned = xt[pl.ds(start, 16), :]
    for level in range(4):
        sep_out[0, level] = turned[0:8, 16 * level : 16 * level + 16]
        sep_out[1, level] = -turned[8:16, 16 * level : 16 * level + 16]
    arrive("g6")
    arrive("g5")
    arrive("g4")
    for level, size, first, ref in ((7, 8, 0, g6g), (6, 4, quad, g5g), (5, 2, pair, g4g)):
        want = (16 * (leaf - 16 * first) + iota((16, 256), 0)).astype(f32)
        block = jnp.zeros((16, 16), f32)
        for s in range(size):
            block = block + mm_nt(hot(want == dl_[first + s][level - 1 : level]), ref[s])
        sep_out[0, level - 1] = block[0:8]
        sep_out[1, level - 1] = -block[8:16]

    for one in pending:
        one.wait_send()


def body(leaf_rhs, sep_rhs, leaf_inv, leaf_low, sep_inv, sep_low, leaf_live, targets):
    vm = pl.BlockSpec(memory_space=pltpu.VMEM)
    hb = pl.BlockSpec(memory_space=pltpu.HBM)
    sm = pl.BlockSpec(memory_space=pltpu.SMEM)
    V = pltpu.VMEM

    def rows(*lead):
        return V(lead + (16, 256), bf16)

    def squares(count):
        return V((count, 256, 256), bf16)

    out_leaf, out_sep = pl.pallas_call(
        kernel,
        out_shape=(
            jax.ShapeDtypeStruct((2, 16, 512), f32),
            jax.ShapeDtypeStruct((2, 7, 8, 16), f32),
        ),
        in_specs=[hb, hb, hb, hb, hb, hb, hb, sm, sm],
        out_specs=(vm, vm),
        scratch_shapes=[
            V((2, 16, 512), f32), V((2, 7, 8, 16), f32), V((2, 128, 512), bf16),
            V((2, 8, 512), bf16), V((2, 8, 2032), bf16), V((2, 8, 1008), bf16),
            V((7, 128), jnp.int32), pltpu.SemaphoreType.DMA((7,)),
            V((16, 128), f32), V((16, 3072), f32), V((8, 2, 16, 128), bf16),
            V((8, 2, 16, 512), bf16), V((8, 2, 16, 768), bf16),
            V((2, 16, 128), bf16), V((4, 16, 128), bf16), V((8, 16, 128), bf16),
            V((8, 2, 2, 16, 128), bf16), V((8, 2, 4, 16, 128), bf16), V((8, 2, 8, 16, 128), bf16),
            V((4, 2, 16, 128), bf16), V((4, 2, 16, 128), bf16), V((16, 1024), bf16),
            V((8, 8, 256), f32), V((256, 256), bf16), squares(3),
            V((128, 256), f32), rows(4),
            squares(3), V((256, 256), bf16), rows(32), rows(64), rows(128),
            rows(32), rows(64), rows(128), squares(4), squares(2), squares(4),
            rows(2), rows(4), rows(8), rows(2), rows(4), rows(8),
            V((4, 16, 256), f32), V((2, 16, 256), f32), rows(3), rows(3), rows(), rows(),
            rows(8), rows(4), rows(2),
            V((4, 2, 16, 512), bf16), V((3, 2, 16, 512), bf16), V((4, 2, 16, 512), f32),
            V((64, 256), f32), V((256, 64), f32),
            pltpu.SemaphoreType.DMA((COPIES,)), pltpu.SemaphoreType.DMA((COPIES,)),
        ],
        compiler_params=pltpu.CompilerParams(
            collective_id=0, has_side_effects=True, vmem_limit_bytes=60 * 2**20
        ),
    )(
        leaf_rhs, sep_rhs.transpose(0, 2, 3, 1), leaf_inv, leaf_low.transpose(0, 2, 1),
        sep_inv, sep_low, targets, leaf_live, targets,
    )
    return out_leaf, out_sep.transpose(0, 3, 1, 2)


def solution(mesh):
    placed = (
        P(None, "rhs", "leaf"),
        P(None, "rhs", None, "leaf"),
        P(None, "rhs", "leaf"),
        P(None, None, "leaf"),
        P(None, None, "leaf"),
        P(None, None, "leaf"),
        P("leaf"),
        P(),
    )
    return jax.shard_map(
        body,
        mesh=mesh,
        in_specs=placed,
        out_specs=(P(None, "rhs", "leaf"), P(None, "rhs", None, "leaf")),
        check_vma=False,
    )
```

```python
import jax
import jax.numpy as jnp
from jax import lax
from jax.experimental import pallas as pl
from jax.experimental.pallas import tpu as pltpu
from jax.sharding import PartitionSpec as P

MESH = pl.DeviceIdType.MESH
bf16 = jnp.bfloat16
f32 = jnp.float32

COUNTS = dict(
    msg=15, zx=3, c0=7, c4=7, q1=1, q2=3, q3=7, c1=7, c2=7, c3=7, t0=1, t1=1, t2=1, t3=1, t4=1,
    x2=3, x3=3, x4=3, h=7, u4=1, u5=3, u6=7, d6=3, d5=1, g6=7, g5=3, lw=3,
)
FIRST = {}
_total = 0
for _name, _count in COUNTS.items():
    FIRST[_name] = _total
    _total += _count
COPIES = _total


def mm(a, b):
    return jnp.dot(a, b, preferred_element_type=f32)


def mm_nt(a, b):
    return lax.dot_general(a, b, (((1,), (1,)), ((), ())), preferred_element_type=f32)


def flip(value, mask):
    out = value
    for bit in range(3):
        if mask >> bit & 1:
            here = lax.rem(lax.div(value, 1 << bit), 2)
            out = out + (1 - 2 * here) * (1 << bit)
    return out


def iota(shape, axis):
    return lax.broadcasted_iota(jnp.int32, shape, axis)


def hot(test):
    return test.astype(f32).astype(bf16)


def kernel(
    rhs_hbm, sep_hbm, inv_hbm, low_hbm, sinv_hbm, slow_hbm, tgt_hbm, live_ref, tgs,
    leaf_out, sep_out,
    rhs_ref, sep_ref, inv_ref, low_ref, sinv_ref, slow_ref, tgt_ref, lsem,
    st, pk, m0, c0, c4, p1, p2, p3, p4, z2, z3, c1, c2, c3, zxs, zxr, eh, dl_, p0, pis, rs_, vs,
    m123, b4, b5, b6, b7, n5, n6, n7, i14, i5, i6, hh, u4g, u5g, u6g,
    wq6, wq5, d6s, d6r, d5s, d5r, g6g, g5g, g4g, lws, lwr, lwo, xo, xt, ssem, rsem,
):
    loads = []
    for j, (src, dst) in enumerate((
        (rhs_hbm, rhs_ref), (low_hbm, low_ref), (sep_hbm, sep_ref), (slow_hbm, slow_ref),
        (sinv_hbm, sinv_ref), (tgt_hbm, tgt_ref), (inv_hbm, inv_ref),
    )):
        loads.append(pltpu.make_async_copy(src, dst, lsem.at[j]))
        loads[-1].start()
    leaf = lax.axis_index("leaf")
    x = lax.axis_index("rhs")
    c = lax.rem(leaf, 2)
    y = lax.rem(lax.div(leaf, 2), 8)
    z = lax.div(leaf, 16)
    dl = lax.rem(leaf, 16)
    zq = lax.rem(z, 4)
    zp = lax.rem(z, 2)
    quad = z - zq
    pair = z - zp

    def dev(zz, yy, cc, xx):
        return (zz * 16 + yy * 2 + cc, xx)

    layer = [(k >> 1, k & 1) for k in range(1, 16)]
    barrier = pltpu.get_barrier_semaphore()

    def greet(device):
        pl.semaphore_signal(barrier, inc=1, device_id=device, device_id_type=MESH)

    for ky, kc in layer:
        greet(dev(z, flip(y, ky), flip(c, kc), x))
    for k in range(1, 8):
        greet(dev(flip(z, k), y, c, x))
    for k in range(1, 4):
        greet(dev(z, y, c, flip(x, k)))

    pending = []
    got = {name: [] for name in COUNTS}

    def send(name, src, dst, device):
        index = FIRST[name] + len(got[name])
        out = pltpu.make_async_remote_copy(
            src_ref=src, dst_ref=dst, send_sem=ssem.at[index], recv_sem=rsem.at[index],
            device_id=device, device_id_type=MESH,
        )
        out.start()
        pending.append(out)
        got[name].append(out)

    def arrive(name):
        for one in got[name]:
            one.wait_recv()

    def scatter(name, buf):
        for k in range(1, 8):
            send(name, buf.at[y, c], buf.at[y, c], dev(z, flip(y, k), c, x))

    def quarter(name, buf):
        for k in range(1, 8):
            send(name, buf.at[y, c, x], buf.at[y, c, x], dev(z, flip(y, k), c, x))

    def planes(name, tag, buf):
        arrive(name)
        for k in range(1, 4):
            send(tag, buf.at[:, c, x], buf.at[:, c, x], dev(z, y, c, flip(x, k)))

    def twin(name, tag, buf):
        arrive(name)
        send(tag, buf.at[:, c], buf.at[:, c], dev(z, y, 1 - c, x))

    def along(name, count, buf, slot):
        for k in range(1, count):
            send(name, buf.at[slot], buf.at[slot], dev(flip(z, k), y, c, x))

    loads[0].wait()
    loads[1].wait()
    live = live_ref[0]
    mask = iota((1, 512), 1) < live * 128
    zr = jnp.where(mask, rhs_ref[0], 0.0).astype(bf16)
    zi = jnp.where(mask, rhs_ref[1], 0.0).astype(bf16)
    er = low_ref[0].astype(f32)
    ei = low_ref[1].astype(f32)
    ehv = jnp.concatenate(
        [jnp.concatenate([er, -ei], axis=1), jnp.concatenate([ei, er], axis=1)], axis=0
    ).astype(bf16)
    eh[...] = ehv
    zcat = jnp.concatenate([zr, zi], axis=1)
    st[:, 112:128] = mm_nt(ehv, zcat)
    loads[2].wait()
    for level in range(7):
        st[0:8, 16 * level : 16 * level + 16] = sep_ref[0, level]
        st[8:16, 16 * level : 16 * level + 16] = sep_ref[1, level]
    m0[y, c] = st[...].astype(bf16)
    pk[:, 0:128] = jnp.zeros((16, 128), f32)
    pk[:, 1024:1152] = jnp.zeros((16, 128), f32)
    loads[3].wait()
    loads[4].wait()
    for part in range(2):
        pk[8 * part : 8 * part + 8, 16:1024] = slow_ref[part].astype(f32)
        pk[8 * part : 8 * part + 8, 1040:3072] = sinv_ref[part].astype(f32)
    c0[y, c] = pk[:, 0:256].astype(bf16)
    for t in range(4):
        p4[t] = pk[:, 1024 + 256 * t : 1280 + 256 * t].astype(bf16)
    c4[y, c, x] = p4[x]
    for q in range(4):
        zxs[q, 0] = zr[:, 128 * q : 128 * q + 128]
        zxs[q, 1] = zi[:, 128 * q : 128 * q + 128]
    zxr[x] = zxs[x]
    for t in range(2):
        p1[t] = pk[:, 256 + 128 * t : 384 + 128 * t].astype(bf16)
    for t in range(4):
        p2[t] = pk[:, 512 + 128 * t : 640 + 128 * t].astype(bf16)
    c1[y, c, zp] = p1[zp]
    z2[zq] = p2[zq]
    loads[5].wait()
    tgt = tgt_ref[...].astype(f32).astype(bf16)
    spot = iota((128, 1024), 1)
    wide = mm(tgt, hot(iota((128, 1024), 0) == spot // 8))
    place = 8.0 * wide[6:7] + (iota((1, 1024), 1) % 8).astype(f32)
    top_rows = pk[:, 2048:3072].astype(bf16)
    down = iota((1024, 256), 0).astype(f32)
    for t in range(4):
        moved = mm(top_rows, hot(down == place[:, 256 * t : 256 * t + 256])).astype(bf16)
        p3[2 * t] = moved[:, 0:128]
        p3[2 * t + 1] = moved[:, 128:256]
    z3[lax.div(z, 2), zp] = p3[z]

    pl.semaphore_wait(barrier, 25)

    for ky, kc in layer:
        send("msg", m0.at[y, c], m0.at[y, c], dev(z, flip(y, ky), flip(c, kc), x))
    scatter("c0", c0)
    send("q1", p1.at[1 - zp], c1.at[y, c, zp], dev(flip(z, 1), y, c, x))
    for k in range(1, 4):
        send("q2", p2.at[flip(zq, k)], z2.at[zq], dev(flip(z, k), y, c, x))
    for k in range(1, 8):
        send("q3", p3.at[flip(z, k)], z3.at[lax.div(z, 2), zp], dev(flip(z, k), y, c, x))
    quarter("c4", c4)
    for k in range(1, 4):
        send("zx", zxs.at[flip(x, k)], zxr.at[x], dev(z, y, c, flip(x, k)))

    lane16 = (iota((1, 256), 1) % 16).astype(f32)
    for s in range(8):
        pick = iota((128, 256), 0) == 16 * s + iota((128, 256), 1) // 16
        dl_[s, 0:7] = 16.0 * mm(tgt, hot(pick)) + lane16
    down = iota((256, 256), 0).astype(f32)

    def route(level, source, slab):
        shift = jnp.asarray(256 * slab, jnp.int32).astype(f32)
        return hot(down + shift == dl_[source][level : level + 1])

    p0[...] = hot(down == dl_[z][0:1] + (iota((1, 256), 1) // 32 * 32).astype(f32))
    lane = iota((1, 256), 1)
    pick = iota((128, 256), 0) == 16 * z + iota((128, 256), 1) % 128 // 8
    inner = (lane // 128 * 8 + lane % 8).astype(f32)
    old = 16.0 * mm(tgt, hot(pick)) + inner
    for level in range(1, 4):
        base = (lane % 128 // 8 // (2 << level) * (2 << level) * 16).astype(f32)
        pis[level - 1] = hot(down == old[level : level + 1] + base)
    rown = iota((256, 1), 0)
    natural = hot(iota((256, 256), 1) == rown % 128 // 8 * 16 + rown // 128 * 8 + rown % 8)
    sign_row = (1 - 2 * (iota((256, 1), 0) // 8 % 2)).astype(f32)
    sign_lane = (1 - 2 * (lane // 8 % 2)).astype(f32)

    def embed(raw):
        parts = raw.reshape(16, 2, 8, 128)
        swapped = jnp.concatenate([parts[:, 1:2], parts[:, 0:1]], axis=1).reshape(256, 128)
        return jnp.concatenate([raw * sign_row, swapped], axis=1).astype(bf16)

    def square(raw):
        return mm(embed(raw.reshape(256, 128).astype(f32)), natural).astype(bf16)

    def small(raw, level):
        size = 8 << level
        at = iota((128, 128), 0)
        to = iota((128, 128), 1)
        repeat = hot(at == size + to % size)
        spread = mm(raw, repeat)
        front = iota((256, 128), 0) // (16 << level) == iota((256, 128), 1) // size
        return embed(jnp.where(front, spread, 0.0))

    def blocks(ref, s):
        return ref[pl.ds(16 * s, 16)].reshape(256, 256)

    arrive("msg")
    flipped = jnp.transpose(m0[...].reshape(256, 128).astype(f32))
    rs_[...] = flipped
    u = mm_nt(flipped[112:128].astype(bf16), p0[...])
    v = (flipped[0:16] - u).astype(bf16)
    vs[0] = v
    twin("c0", "t0", c0)
    arrive("q1")
    scatter("c1", c1)
    arrive("q2")
    c2[y, c, x] = z2[x]
    quarter("c2", c2)
    arrive("t0")
    raw0 = c0[:, :, :, 0:128].reshape(256, 128)
    for level in range(1, 4):
        m123[level - 1] = mm_nt(small(raw0, level), pis[level - 1]).astype(bf16)
        u = mm(v, m123[level - 1])
        v = (rs_[16 * level : 16 * level + 16] - u).astype(bf16)
        vs[level] = v
    b4[...] = square(c0[:, :, :, 128:256])
    own = mm(v, b4[...]).astype(bf16)
    u4g[zp] = own
    along("u4", 2, u4g, zp)
    hh[z, 0] = rs_[96:112].astype(bf16)
    hh[z, 1] = rs_[80:96].astype(bf16)
    hh[z, 2] = rs_[64:80].astype(bf16)
    for k in range(1, 8):
        part = pl.ds(0, 3 if k < 2 else 2 if k < 4 else 1)
        send("h", hh.at[z, part], hh.at[z, part], dev(flip(z, k), y, c, x))
    arrive("q3")
    c3[y, c, x] = z3[x]
    quarter("c3", c3)

    twin("c1", "t1", c1)
    planes("c4", "x4", c4)
    arrive("zx")
    loads[6].wait()
    zr4 = zxr[:, 0].reshape(64, 128)
    zi4 = zxr[:, 1].reshape(64, 128)
    panel = inv_ref[...].reshape(256, 512)
    real = mm(jnp.concatenate([zr4, -zi4], axis=1), panel).reshape(4, 16, 512)
    imag = mm(jnp.concatenate([zi4, zr4], axis=1), panel).reshape(4, 16, 512)
    lwo[:, 0] = real
    lwo[:, 1] = imag
    lws[:, 0] = real.astype(bf16)
    lws[:, 1] = imag.astype(bf16)
    for k in range(1, 4):
        send("lw", lws.at[flip(x, k)], lwr.at[k - 1], dev(z, y, c, flip(x, k)))
    planes("c2", "x2", c2)
    arrive("t1")
    for s in range(2):
        b5[16 * s : 16 * s + 16] = square(c1[:, :, s]).reshape(16, 16, 256)

    def move(level, first, source, target):
        def step(i, carry):
            target[i] = source[tgs[level, first + i]]
            return carry
        return step

    lax.fori_loop(0, 32, move(4, 16 * pair, b5, n5), 0, unroll=8)
    got["h"][0].wait_recv()
    u = -mm(own, blocks(n5, zp))
    for s in range(2):
        u = u + mm(hh[pair + s, 2], blocks(b5, s))
    arrive("u4")
    u = u - mm(u4g[1 - zp], blocks(n5, 1 - zp))
    own = u.astype(bf16)
    u5g[zq] = own
    along("u5", 4, u5g, zq)

    twin("x2", "t2", c2)
    planes("c3", "x3", c3)
    arrive("t2")
    for s in range(4):
        b6[16 * s : 16 * s + 16] = square(c2[:, :, s]).reshape(16, 16, 256)
    lax.fori_loop(0, 64, move(5, 16 * quad, b6, n6), 0, unroll=8)
    got["h"][1].wait_recv()
    got["h"][2].wait_recv()
    u = -mm(own, blocks(n6, zq))
    for s in range(4):
        u = u + mm(hh[quad + s, 1], blocks(b6, s))
    for k in range(1, 4):
        got["u5"][k - 1].wait_recv()
        u = u - mm(u5g[flip(zq, k)], blocks(n6, flip(zq, k)))
    own = u.astype(bf16)
    u6g[z] = own
    along("u6", 8, u6g, z)

    twin("x3", "t3", c3)
    twin("x4", "t4", c4)
    arrive("t3")
    for s in range(8):
        b7[16 * s : 16 * s + 16] = square(c3[:, :, s // 2, s % 2]).reshape(16, 16, 256)
    lax.fori_loop(0, 128, move(6, 0, b7, n7), 0, unroll=8)
    for k in range(3, 7):
        got["h"][k].wait_recv()
    u = -mm(own, blocks(n7, z))
    for s in range(8):
        u = u + mm(hh[s, 0], blocks(b7, s))

    arrive("t4")
    v5 = rs_[64:80]
    for s in range(2):
        i5[s] = square(c4[:, :, 1, :, 128 * s : 128 * s + 128])
        v5 = v5 - mm_nt(u4g[s], route(4, pair + s, zp))
    v5 = v5.astype(bf16)
    v6 = rs_[80:96]
    for s in range(4):
        i6[s] = square(c4[:, :, 2 + s // 2, :, 128 * (s % 2) : 128 * (s % 2) + 128])
        v6 = v6 - mm_nt(u5g[s], route(5, quad + s, zq))
    v6 = v6.astype(bf16)
    w6 = [mm(v6, i6[s]).astype(bf16) for s in range(4)]
    for s in range(4):
        total = mm(w6[0], route(5, quad + s, 0))
        for t in range(1, 4):
            total = total + mm(w6[t], route(5, quad + s, t))
        wq6[s] = total * sign_lane

    for k in range(1, 8):
        got["u6"][k - 1].wait_recv()
        u = u - mm(u6g[flip(z, k)], blocks(n7, flip(z, k)))
    own = (u * sign_lane).astype(bf16)

    for k in range(1, 4):
        t = flip(zq, k)
        d6s[k - 1] = (wq6[t] - mm_nt(own, blocks(n6, t))).astype(bf16)
        send("d6", d6s.at[k - 1], d6r.at[k - 1], dev(flip(z, k), y, c, x))
    below = wq6[zq] - mm_nt(own, blocks(n6, zq))
    g6g[z] = own
    along("g6", 8, g6g, z)

    w5 = [mm(v5, i5[s]).astype(bf16) for s in range(2)]
    for s in range(2):
        wq5[s] = sign_lane * (
            mm(w5[0], route(4, pair + s, 0)) + mm(w5[1], route(4, pair + s, 1))
        )
    rawi = c4[:, :, 0, :, 0:128].reshape(256, 128)
    for level in range(1, 4):
        i14[level - 1] = mm(small(rawi, level), natural).astype(bf16)
    i14[3] = square(c4[:, :, 0, :, 128:256])
    for level in range(1, 5):
        xo[16 * level - 16 : 16 * level] = mm(vs[level - 1], i14[level - 1]) * sign_lane

    arrive("d6")
    for k in range(3):
        below = below + d6r[k].astype(f32)
    own = below.astype(bf16)
    below = [wq5[s] - mm_nt(own, blocks(n5, s)) for s in range(2)]
    for s in range(2):
        d5s[s] = below[s].astype(bf16)
    send("d5", d5s, d5r, dev(flip(z, 1), y, c, x))
    g5g[zq] = own
    along("g5", 4, g5g, zq)

    def emit(level, size, first, ref):
        want = (16 * (leaf - 16 * first) + iota((16, 256), 0)).astype(f32)
        block = jnp.zeros((16, 16), f32)
        for s in range(size):
            block = block + mm_nt(hot(want == dl_[first + s][level - 1 : level]), ref[s])
        sep_out[0, level - 1] = block[0:8]
        sep_out[1, level - 1] = -block[8:16]

    arrive("g6")
    emit(7, 8, 0, g6g)
    arrive("d5")
    for s in range(2):
        g4g[s] = (below[s] + d5r[s].astype(f32)).astype(bf16)
    own = g4g[zp]
    now = xo[48:64] - mm_nt(own, b4[...])
    xo[48:64] = now
    for level in range(3, 0, -1):
        now = xo[16 * level - 16 : 16 * level] - mm_nt(now.astype(bf16), m123[level - 1])
        xo[16 * level - 16 : 16 * level] = now
    parent = 16 * (dl - c + tgs[0, leaf])
    chosen = hot(iota((16, 256), 1) == parent + iota((16, 256), 0))
    back = mm_nt(now.astype(bf16), chosen).astype(bf16)
    less = mm(back, eh[...])
    arrive("lw")
    mine = lwo[x]
    for k in range(3):
        mine = mine + lwr[k].astype(f32)
    leaf_out[0] = jnp.where(mask, mine[0] - less[:, 0:512], 0.0)
    leaf_out[1] = jnp.where(mask, mine[1] + less[:, 512:1024], 0.0)

    xt[...] = jnp.transpose(xo[...])
    start = pl.multiple_of(dl * 16, 16)
    turned = xt[pl.ds(start, 16), :]
    for level in range(4):
        sep_out[0, level] = turned[0:8, 16 * level : 16 * level + 16]
        sep_out[1, level] = -turned[8:16, 16 * level : 16 * level + 16]
    arrive("g5")
    emit(6, 4, quad, g5g)
    emit(5, 2, pair, g4g)

    for one in pending:
        one.wait_send()


def body(leaf_rhs, sep_rhs, leaf_inv, leaf_low, sep_inv, sep_low, leaf_live, targets):
    vm = pl.BlockSpec(memory_space=pltpu.VMEM)
    hb = pl.BlockSpec(memory_space=pltpu.HBM)
    sm = pl.BlockSpec(memory_space=pltpu.SMEM)
    V = pltpu.VMEM

    def rows(*lead):
        return V(lead + (16, 256), bf16)

    def squares(count):
        return V((count, 256, 256), bf16)

    out_leaf, out_sep = pl.pallas_call(
        kernel,
        out_shape=(
            jax.ShapeDtypeStruct((2, 16, 512), f32),
            jax.ShapeDtypeStruct((2, 7, 8, 16), f32),
        ),
        in_specs=[hb, hb, hb, hb, hb, hb, hb, sm, sm],
        out_specs=(vm, vm),
        scratch_shapes=[
            V((2, 16, 512), f32), V((2, 7, 8, 16), f32), V((2, 128, 512), bf16),
            V((2, 8, 512), bf16), V((2, 8, 2032), bf16), V((2, 8, 1008), bf16),
            V((7, 128), jnp.int32), pltpu.SemaphoreType.DMA((7,)),
            V((16, 128), f32), V((16, 3072), f32), V((8, 2, 16, 128), bf16),
            V((8, 2, 16, 256), bf16), V((8, 2, 4, 16, 256), bf16),
            V((2, 16, 128), bf16), V((4, 16, 128), bf16), V((8, 16, 128), bf16), rows(4),
            V((4, 16, 128), bf16), V((4, 2, 16, 128), bf16),
            V((8, 2, 2, 16, 128), bf16), V((8, 2, 4, 16, 128), bf16), V((8, 2, 4, 2, 16, 128), bf16),
            V((4, 2, 16, 128), bf16), V((4, 2, 16, 128), bf16), V((16, 1024), bf16),
            V((8, 8, 256), f32), V((256, 256), bf16), squares(3),
            V((128, 256), f32), rows(4),
            squares(3), V((256, 256), bf16), rows(32), rows(64), rows(128),
            rows(32), rows(64), rows(128), squares(4), squares(2), squares(4),
            rows(8, 3), rows(2), rows(4), rows(8),
            V((4, 16, 256), f32), V((2, 16, 256), f32), rows(3), rows(3), rows(2), rows(2),
            rows(8), rows(4), rows(2),
            V((4, 2, 16, 512), bf16), V((3, 2, 16, 512), bf16), V((4, 2, 16, 512), f32),
            V((64, 256), f32), V((256, 64), f32),
            pltpu.SemaphoreType.DMA((COPIES,)), pltpu.SemaphoreType.DMA((COPIES,)),
        ],
        compiler_params=pltpu.CompilerParams(
            collective_id=0, has_side_effects=True, vmem_limit_bytes=60 * 2**20
        ),
    )(
        leaf_rhs, sep_rhs.transpose(0, 2, 3, 1), leaf_inv, leaf_low.transpose(0, 2, 1),
        sep_inv, sep_low, targets, leaf_live, targets,
    )
    return out_leaf, out_sep.transpose(0, 3, 1, 2)


def solution(mesh):
    placed = (
        P(None, "rhs", "leaf"),
        P(None, "rhs", None, "leaf"),
        P(None, "rhs", "leaf"),
        P(None, None, "leaf"),
        P(None, None, "leaf"),
        P(None, None, "leaf"),
        P("leaf"),
        P(),
    )
    return jax.shard_map(
        body,
        mesh=mesh,
        in_specs=placed,
        out_specs=(P(None, "rhs", "leaf"), P(None, "rhs", None, "leaf")),
        check_vma=False,
    )
```

```python
import jax
import jax.numpy as jnp
from jax import lax
from jax.experimental import pallas as pl
from jax.experimental.pallas import tpu as pltpu
from jax.sharding import PartitionSpec as P

MESH = pl.DeviceIdType.MESH
bf16 = jnp.bfloat16
f32 = jnp.float32

COUNTS = dict(
    msg=15, zx=3, c0=7, c4=7, q1=1, q2=3, q3=7, c1=7, c2=7, c3=7, t0=1, t1=1, t2=1, t3=1, t4=1,
    x2=3, x3=3, x4=3, h=7, u4=1, u5=3, u6=7, d6=3, d5=1, g6=7, e6=3, lw=3,
)
FIRST = {}
_total = 0
for _name, _count in COUNTS.items():
    FIRST[_name] = _total
    _total += _count
COPIES = _total


def mm(a, b):
    return jnp.dot(a, b, preferred_element_type=f32)


def mm_nt(a, b):
    return lax.dot_general(a, b, (((1,), (1,)), ((), ())), preferred_element_type=f32)


def flip(value, mask):
    out = value
    for bit in range(3):
        if mask >> bit & 1:
            here = lax.rem(lax.div(value, 1 << bit), 2)
            out = out + (1 - 2 * here) * (1 << bit)
    return out


def iota(shape, axis):
    return lax.broadcasted_iota(jnp.int32, shape, axis)


def hot(test):
    return test.astype(f32).astype(bf16)


def kernel(
    rhs_hbm, sep_hbm, inv_hbm, low_hbm, sinv_hbm, slow_hbm, tgt_hbm, live_ref,
    leaf_out, sep_out,
    rhs_ref, sep_ref, inv_ref, low_ref, sinv_ref, slow_ref, tgt_ref, tgs, lsem,
    st, pk, m0, c0, c4, p1, p2, p3, p4, z2, z3, c1, c2, c3, zxs, zxr, eh, dl_, p0, pis, rs_, vs,
    m123, b4, b5, b6, b7, n5, n6, n7, i14, i5, i6, hh, u4g, u5g, u6g,
    wq6, wq5, wn6, e6s, e6r, d6s, d6r, d5s, d5r, g6g, g4g, lws, lwr, lwo, xo, xt, ssem, rsem,
):
    loads = []
    for j, (src, dst) in enumerate((
        (rhs_hbm, rhs_ref), (low_hbm, low_ref), (sep_hbm, sep_ref), (slow_hbm, slow_ref),
        (sinv_hbm, sinv_ref), (tgt_hbm, tgt_ref), (inv_hbm, inv_ref), (tgt_hbm, tgs),
    )):
        loads.append(pltpu.make_async_copy(src, dst, lsem.at[j]))
        loads[-1].start()
    leaf = lax.axis_index("leaf")
    x = lax.axis_index("rhs")
    c = lax.rem(leaf, 2)
    y = lax.rem(lax.div(leaf, 2), 8)
    z = lax.div(leaf, 16)
    dl = lax.rem(leaf, 16)
    zq = lax.rem(z, 4)
    zp = lax.rem(z, 2)
    quad = z - zq
    pair = z - zp

    def dev(zz, yy, cc, xx):
        return (zz * 16 + yy * 2 + cc, xx)

    layer = [(ky, kc) for ky in (4, 3, 5, 2, 6, 7, 1, 0) for kc in (0, 1) if ky or kc]
    barrier = pltpu.get_barrier_semaphore()

    def greet(device):
        pl.semaphore_signal(barrier, inc=1, device_id=device, device_id_type=MESH)

    far = (4, 3, 5, 2, 6, 7, 1)
    for k in far:
        greet(dev(flip(z, k), y, c, x))
        greet(dev(z, flip(y, k), c, x))
        greet(dev(z, flip(y, k), 1 - c, x))
    for k in (2, 1, 3):
        greet(dev(z, y, c, flip(x, k)))
    greet(dev(z, y, 1 - c, x))

    pending = []
    got = {name: [] for name in COUNTS}

    def send(name, src, dst, device):
        index = FIRST[name] + len(got[name])
        out = pltpu.make_async_remote_copy(
            src_ref=src, dst_ref=dst, send_sem=ssem.at[index], recv_sem=rsem.at[index],
            device_id=device, device_id_type=MESH,
        )
        out.start()
        pending.append(out)
        got[name].append(out)

    def arrive(name):
        for one in got[name]:
            one.wait_recv()

    def scatter(name, buf):
        for k in range(1, 8):
            send(name, buf.at[y, c], buf.at[y, c], dev(z, flip(y, k), c, x))

    def quarter(name, buf):
        for k in range(1, 8):
            send(name, buf.at[y, c, x], buf.at[y, c, x], dev(z, flip(y, k), c, x))

    def planes(name, tag, buf):
        arrive(name)
        for k in range(1, 4):
            send(tag, buf.at[:, c, x], buf.at[:, c, x], dev(z, y, c, flip(x, k)))

    def twin(name, tag, buf):
        arrive(name)
        send(tag, buf.at[:, c], buf.at[:, c], dev(z, y, 1 - c, x))

    def along(name, count, buf, slot):
        for k in range(1, count):
            send(name, buf.at[slot], buf.at[slot], dev(flip(z, k), y, c, x))

    loads[0].wait()
    loads[1].wait()
    live = live_ref[0]
    mask = iota((1, 512), 1) < live * 128
    zr = jnp.where(mask, rhs_ref[0], 0.0).astype(bf16)
    zi = jnp.where(mask, rhs_ref[1], 0.0).astype(bf16)
    er = low_ref[0].astype(f32)
    ei = low_ref[1].astype(f32)
    ehv = jnp.concatenate(
        [jnp.concatenate([er, -ei], axis=1), jnp.concatenate([ei, er], axis=1)], axis=0
    ).astype(bf16)
    eh[...] = ehv
    zcat = jnp.concatenate([zr, zi], axis=1)
    st[:, 112:128] = mm_nt(ehv, zcat)
    loads[2].wait()
    for level in range(7):
        st[0:8, 16 * level : 16 * level + 16] = sep_ref[0, level]
        st[8:16, 16 * level : 16 * level + 16] = sep_ref[1, level]
    m0[y, c] = st[...].astype(bf16)
    pk[:, 0:128] = jnp.zeros((16, 128), f32)
    pk[:, 1024:1152] = jnp.zeros((16, 128), f32)
    loads[3].wait()
    loads[4].wait()
    for part in range(2):
        pk[8 * part : 8 * part + 8, 16:1024] = slow_ref[part].astype(f32)
        pk[8 * part : 8 * part + 8, 1040:3072] = sinv_ref[part].astype(f32)
    c0[y, c] = pk[:, 0:256].astype(bf16)
    for t in range(4):
        p4[t] = pk[:, 1024 + 256 * t : 1280 + 256 * t].astype(bf16)
    c4[y, c, x] = p4[x]
    for q in range(4):
        zxs[q, 0] = zr[:, 128 * q : 128 * q + 128]
        zxs[q, 1] = zi[:, 128 * q : 128 * q + 128]
    zxr[x] = zxs[x]
    for t in range(2):
        p1[t] = pk[:, 256 + 128 * t : 384 + 128 * t].astype(bf16)
    for t in range(4):
        p2[t] = pk[:, 512 + 128 * t : 640 + 128 * t].astype(bf16)
    c1[y, c, zp] = p1[zp]
    z2[zq] = p2[zq]
    loads[5].wait()
    loads[7].wait()
    tgt = tgt_ref[...].astype(f32).astype(bf16)
    spot = iota((128, 1024), 1)
    wide = mm(tgt, hot(iota((128, 1024), 0) == spot // 8))
    place = 8.0 * wide[6:7] + (iota((1, 1024), 1) % 8).astype(f32)
    top_rows = pk[:, 2048:3072].astype(bf16)
    down = iota((1024, 256), 0).astype(f32)
    for t in range(4):
        moved = mm(top_rows, hot(down == place[:, 256 * t : 256 * t + 256])).astype(bf16)
        p3[2 * t] = moved[:, 0:128]
        p3[2 * t + 1] = moved[:, 128:256]
    z3[lax.div(z, 2), zp] = p3[z]

    pl.semaphore_wait(barrier, 25)

    scatter("c0", c0)
    for ky, kc in layer:
        send("msg", m0.at[y, c], m0.at[y, c], dev(z, flip(y, ky), flip(c, kc), x))
    send("q1", p1.at[1 - zp], c1.at[y, c, zp], dev(flip(z, 1), y, c, x))
    for k in range(1, 4):
        send("q2", p2.at[flip(zq, k)], z2.at[zq], dev(flip(z, k), y, c, x))
    for k in range(1, 8):
        send("q3", p3.at[flip(z, k)], z3.at[lax.div(z, 2), zp], dev(flip(z, k), y, c, x))
    for k in range(1, 4):
        send("zx", zxs.at[flip(x, k)], zxr.at[x], dev(z, y, c, flip(x, k)))

    lane16 = (iota((1, 256), 1) % 16).astype(f32)
    for s in range(8):
        pick = iota((128, 256), 0) == 16 * s + iota((128, 256), 1) // 16
        dl_[s, 0:7] = 16.0 * mm(tgt, hot(pick)) + lane16
    down = iota((256, 256), 0).astype(f32)

    def route(level, source, slab):
        shift = jnp.asarray(256 * slab, jnp.int32).astype(f32)
        return hot(down + shift == dl_[source][level : level + 1])

    p0[...] = hot(down == dl_[z][0:1] + (iota((1, 256), 1) // 32 * 32).astype(f32))
    lane = iota((1, 256), 1)
    pick = iota((128, 256), 0) == 16 * z + iota((128, 256), 1) % 128 // 8
    inner = (lane // 128 * 8 + lane % 8).astype(f32)
    old = 16.0 * mm(tgt, hot(pick)) + inner
    for level in range(1, 4):
        base = (lane % 128 // 8 // (2 << level) * (2 << level) * 16).astype(f32)
        pis[level - 1] = hot(down == old[level : level + 1] + base)
    rown = iota((256, 1), 0)
    natural = hot(iota((256, 256), 1) == rown % 128 // 8 * 16 + rown // 128 * 8 + rown % 8)
    sign_row = (1 - 2 * (iota((256, 1), 0) // 8 % 2)).astype(f32)
    sign_lane = (1 - 2 * (lane // 8 % 2)).astype(f32)

    def embed(raw):
        parts = raw.reshape(16, 2, 8, 128)
        swapped = jnp.concatenate([parts[:, 1:2], parts[:, 0:1]], axis=1).reshape(256, 128)
        return jnp.concatenate([raw * sign_row, swapped], axis=1).astype(bf16)

    def square(raw):
        return mm(embed(raw.reshape(256, 128).astype(f32)), natural).astype(bf16)

    def small(raw, level):
        size = 8 << level
        at = iota((128, 128), 0)
        to = iota((128, 128), 1)
        repeat = hot(at == size + to % size)
        spread = mm(raw, repeat)
        front = iota((256, 128), 0) // (16 << level) == iota((256, 128), 1) // size
        return embed(jnp.where(front, spread, 0.0))

    def blocks(ref, s):
        return ref[pl.ds(16 * s, 16)].reshape(256, 256)

    arrive("q1")
    scatter("c1", c1)
    twin("c0", "t0", c0)
    arrive("q2")
    c2[y, c, x] = z2[x]
    quarter("c2", c2)
    arrive("q3")
    c3[y, c, x] = z3[x]
    quarter("c3", c3)
    arrive("msg")
    flipped = jnp.transpose(m0[...].reshape(256, 128).astype(f32))
    rs_[...] = flipped
    u = mm_nt(flipped[112:128].astype(bf16), p0[...])
    v = (flipped[0:16] - u).astype(bf16)
    vs[0] = v
    arrive("t0")
    raw0 = c0[:, :, :, 0:128].reshape(256, 128)
    for level in range(1, 4):
        m123[level - 1] = mm_nt(small(raw0, level), pis[level - 1]).astype(bf16)
        u = mm(v, m123[level - 1])
        v = (rs_[16 * level : 16 * level + 16] - u).astype(bf16)
        vs[level] = v
    b4[...] = square(c0[:, :, :, 128:256])
    own = mm(v, b4[...]).astype(bf16)
    u4g[zp] = own
    along("u4", 2, u4g, zp)
    hh[z, 0] = rs_[96:112].astype(bf16)
    hh[z, 1] = rs_[80:96].astype(bf16)
    hh[z, 2] = rs_[64:80].astype(bf16)
    for k in range(1, 8):
        part = pl.ds(0, 3 if k < 2 else 2 if k < 4 else 1)
        send("h", hh.at[z, part], hh.at[z, part], dev(flip(z, k), y, c, x))
    quarter("c4", c4)

    twin("c1", "t1", c1)
    planes("c2", "x2", c2)
    arrive("t1")
    for s in range(2):
        b5[16 * s : 16 * s + 16] = square(c1[:, :, s]).reshape(16, 16, 256)

    def move(level, first, source, target):
        def step(i, carry):
            target[i] = source[tgs[level, first + i]]
            return carry
        return step

    lax.fori_loop(0, 32, move(4, 16 * pair, b5, n5), 0, unroll=8)
    got["h"][0].wait_recv()
    u = -mm(own, blocks(n5, zp))
    for s in range(2):
        u = u + mm(hh[pair + s, 2], blocks(b5, s))
    arrive("u4")
    u = u - mm(u4g[1 - zp], blocks(n5, 1 - zp))
    own = u.astype(bf16)
    u5g[zq] = own
    along("u5", 4, u5g, zq)

    planes("c3", "x3", c3)
    twin("x2", "t2", c2)
    planes("c4", "x4", c4)
    arrive("zx")
    loads[6].wait()
    zr4 = zxr[:, 0].reshape(64, 128)
    zi4 = zxr[:, 1].reshape(64, 128)
    panel = inv_ref[...].reshape(256, 512)
    real = mm(jnp.concatenate([zr4, -zi4], axis=1), panel).reshape(4, 16, 512)
    imag = mm(jnp.concatenate([zi4, zr4], axis=1), panel).reshape(4, 16, 512)
    lwo[:, 0] = real
    lwo[:, 1] = imag
    lws[:, 0] = real.astype(bf16)
    lws[:, 1] = imag.astype(bf16)
    for k in range(1, 4):
        send("lw", lws.at[flip(x, k)], lwr.at[k - 1], dev(z, y, c, flip(x, k)))
    arrive("t2")
    for s in range(4):
        b6[16 * s : 16 * s + 16] = square(c2[:, :, s]).reshape(16, 16, 256)
    lax.fori_loop(0, 64, move(5, 16 * quad, b6, n6), 0, unroll=8)
    got["h"][1].wait_recv()
    got["h"][2].wait_recv()
    u = -mm(own, blocks(n6, zq))
    for s in range(4):
        u = u + mm(hh[quad + s, 1], blocks(b6, s))
    for k in range(1, 4):
        got["u5"][k - 1].wait_recv()
        u = u - mm(u5g[flip(zq, k)], blocks(n6, flip(zq, k)))
    own = u.astype(bf16)
    u6g[z] = own
    along("u6", 8, u6g, z)

    twin("x3", "t3", c3)
    twin("x4", "t4", c4)
    arrive("t3")
    for s in range(8):
        b7[16 * s : 16 * s + 16] = square(c3[:, :, s // 2, s % 2]).reshape(16, 16, 256)
    lax.fori_loop(0, 128, move(6, 0, b7, n7), 0, unroll=8)
    for k in range(3, 7):
        got["h"][k].wait_recv()
    u = -mm(own, blocks(n7, z))
    for s in range(8):
        u = u + mm(hh[s, 0], blocks(b7, s))

    arrive("t4")
    v5 = rs_[64:80]
    for s in range(2):
        i5[s] = square(c4[:, :, 1, :, 128 * s : 128 * s + 128])
        v5 = v5 - mm_nt(u4g[s], route(4, pair + s, zp))
    v5 = v5.astype(bf16)
    v6 = rs_[80:96]
    for s in range(4):
        i6[s] = square(c4[:, :, 2 + s // 2, :, 128 * (s % 2) : 128 * (s % 2) + 128])
        v6 = v6 - mm_nt(u5g[s], route(5, quad + s, zq))
    v6 = v6.astype(bf16)
    w6 = []
    for s in range(4):
        part = mm(v6, i6[s])
        wn6[s] = part * sign_lane
        w6.append(part.astype(bf16))
    for s in range(4):
        total = mm(w6[0], route(5, quad + s, 0))
        for t in range(1, 4):
            total = total + mm(w6[t], route(5, quad + s, t))
        wq6[s] = total * sign_lane

    for k in range(1, 8):
        got["u6"][k - 1].wait_recv()
        u = u - mm(u6g[flip(z, k)], blocks(n7, flip(z, k)))
    own = (u * sign_lane).astype(bf16)

    for k in range(1, 4):
        t = flip(zq, k)
        d6s[k - 1] = (wq6[t] - mm_nt(own, blocks(n6, t))).astype(bf16)
        send("d6", d6s.at[k - 1], d6r.at[k - 1], dev(flip(z, k), y, c, x))
    below = wq6[zq] - mm_nt(own, blocks(n6, zq))
    g6g[z] = own
    along("g6", 8, g6g, z)
    for k in range(1, 4):
        t = flip(zq, k)
        e6s[k - 1] = (wn6[t] - mm_nt(own, blocks(b6, t))).astype(bf16)
        send("e6", e6s.at[k - 1], e6r.at[k - 1], dev(flip(z, k), y, c, x))
    sixth = wn6[zq] - mm_nt(own, blocks(b6, zq))

    w5 = [mm(v5, i5[s]).astype(bf16) for s in range(2)]
    for s in range(2):
        wq5[s] = sign_lane * (
            mm(w5[0], route(4, pair + s, 0)) + mm(w5[1], route(4, pair + s, 1))
        )
    rawi = c4[:, :, 0, :, 0:128].reshape(256, 128)
    for level in range(1, 4):
        i14[level - 1] = mm(small(rawi, level), natural).astype(bf16)
    i14[3] = square(c4[:, :, 0, :, 128:256])
    for level in range(1, 5):
        xo[16 * level - 16 : 16 * level] = mm(vs[level - 1], i14[level - 1]) * sign_lane

    arrive("d6")
    for k in range(3):
        below = below + d6r[k].astype(f32)
    own = below.astype(bf16)
    below = [wq5[s] - mm_nt(own, blocks(n5, s)) for s in range(2)]
    for s in range(2):
        d5s[s] = below[s].astype(bf16)
    send("d5", d5s, d5r, dev(flip(z, 1), y, c, x))

    def emit(level, size, first, ref):
        want = (16 * (leaf - 16 * first) + iota((16, 256), 0)).astype(f32)
        block = jnp.zeros((16, 16), f32)
        for s in range(size):
            block = block + mm_nt(hot(want == dl_[first + s][level - 1 : level]), ref[s])
        sep_out[0, level - 1] = block[0:8]
        sep_out[1, level - 1] = -block[8:16]

    arrive("g6")
    emit(7, 8, 0, g6g)
    arrive("d5")
    for s in range(2):
        g4g[s] = (below[s] + d5r[s].astype(f32)).astype(bf16)
    own = g4g[zp]
    now = xo[48:64] - mm_nt(own, b4[...])
    xo[48:64] = now
    for level in range(3, 0, -1):
        now = xo[16 * level - 16 : 16 * level] - mm_nt(now.astype(bf16), m123[level - 1])
        xo[16 * level - 16 : 16 * level] = now
    parent = 16 * (dl - c + tgs[0, leaf])
    chosen = hot(iota((16, 256), 1) == parent + iota((16, 256), 0))
    back = mm_nt(now.astype(bf16), chosen).astype(bf16)
    less = mm(back, eh[...])
    arrive("lw")
    mine = lwo[x]
    for k in range(3):
        mine = mine + lwr[k].astype(f32)
    leaf_out[0] = jnp.where(mask, mine[0] - less[:, 0:512], 0.0)
    leaf_out[1] = jnp.where(mask, mine[1] + less[:, 512:1024], 0.0)

    arrive("e6")
    for k in range(3):
        sixth = sixth + e6r[k].astype(f32)
    xo[64:80] = sixth
    xo[80:128] = jnp.zeros((48, 256), f32)
    xt[...] = jnp.transpose(xo[...])
    start = pl.multiple_of(dl * 16, 16)
    turned = xt[pl.ds(start, 16), :]
    for row, level in enumerate((0, 1, 2, 3, 5)):
        sep_out[0, level] = turned[0:8, 16 * row : 16 * row + 16]
        sep_out[1, level] = -turned[8:16, 16 * row : 16 * row + 16]
    emit(5, 2, pair, g4g)

    for one in pending:
        one.wait_send()


def body(leaf_rhs, sep_rhs, leaf_inv, leaf_low, sep_inv, sep_low, leaf_live, targets):
    vm = pl.BlockSpec(memory_space=pltpu.VMEM)
    hb = pl.BlockSpec(memory_space=pltpu.HBM)
    sm = pl.BlockSpec(memory_space=pltpu.SMEM)
    V = pltpu.VMEM

    def rows(*lead):
        return V(lead + (16, 256), bf16)

    def squares(count):
        return V((count, 256, 256), bf16)

    out_leaf, out_sep = pl.pallas_call(
        kernel,
        out_shape=(
            jax.ShapeDtypeStruct((2, 16, 512), f32),
            jax.ShapeDtypeStruct((2, 7, 8, 16), f32),
        ),
        in_specs=[hb] * 7 + [sm],
        out_specs=(vm, vm),
        scratch_shapes=[
            V((2, 16, 512), f32), V((2, 7, 8, 16), f32), V((2, 128, 512), bf16),
            V((2, 8, 512), bf16), V((2, 8, 2032), bf16), V((2, 8, 1008), bf16),
            V((7, 128), jnp.int32), pltpu.SMEM((7, 128), jnp.int32),
            pltpu.SemaphoreType.DMA((8,)),
            V((16, 128), f32), V((16, 3072), f32), V((8, 2, 16, 128), bf16),
            V((8, 2, 16, 256), bf16), V((8, 2, 4, 16, 256), bf16),
            V((2, 16, 128), bf16), V((4, 16, 128), bf16), V((8, 16, 128), bf16), rows(4),
            V((4, 16, 128), bf16), V((4, 2, 16, 128), bf16),
            V((8, 2, 2, 16, 128), bf16), V((8, 2, 4, 16, 128), bf16), V((8, 2, 4, 2, 16, 128), bf16),
            V((4, 2, 16, 128), bf16), V((4, 2, 16, 128), bf16), V((16, 1024), bf16),
            V((8, 8, 256), f32), V((256, 256), bf16), squares(3),
            V((128, 256), f32), rows(4),
            squares(3), V((256, 256), bf16), rows(32), rows(64), rows(128),
            rows(32), rows(64), rows(128), squares(4), squares(2), squares(4),
            rows(8, 3), rows(2), rows(4), rows(8),
            V((4, 16, 256), f32), V((2, 16, 256), f32), V((4, 16, 256), f32), rows(3), rows(3), rows(3), rows(3), rows(2), rows(2),
            rows(8), rows(2),
            V((4, 2, 16, 512), bf16), V((3, 2, 16, 512), bf16), V((4, 2, 16, 512), f32),
            V((128, 256), f32), V((256, 128), f32),
            pltpu.SemaphoreType.DMA((COPIES,)), pltpu.SemaphoreType.DMA((COPIES,)),
        ],
        compiler_params=pltpu.CompilerParams(
            collective_id=0, has_side_effects=True, vmem_limit_bytes=40 * 2**20
        ),
    )(
        *(pltpu.with_memory_space_constraint(one, pltpu.HBM) for one in (
            leaf_rhs, sep_rhs.transpose(0, 2, 3, 1), leaf_inv, leaf_low.transpose(0, 2, 1),
            sep_inv, sep_low, targets,
        )),
        leaf_live,
    )
    return out_leaf, out_sep.transpose(0, 3, 1, 2)


def solution(mesh):
    placed = (
        P(None, "rhs", "leaf"),
        P(None, "rhs", None, "leaf"),
        P(None, "rhs", "leaf"),
        P(None, None, "leaf"),
        P(None, None, "leaf"),
        P(None, None, "leaf"),
        P("leaf"),
        P(),
    )
    return jax.shard_map(
        body,
        mesh=mesh,
        in_specs=placed,
        out_specs=(P(None, "rhs", "leaf"), P(None, "rhs", None, "leaf")),
        check_vma=False,
    )
```

```python
import jax
import jax.numpy as jnp
from jax import lax
from jax.experimental import pallas as pl
from jax.experimental.pallas import tpu as pltpu
from jax.sharding import PartitionSpec as P

MESH = pl.DeviceIdType.MESH
bf16 = jnp.bfloat16
f32 = jnp.float32

COUNTS = dict(
    msg=15, zx=3, c0=7, c4=7, c5=7, q0=1, q1=1, q2=3, q3=7, c1=7, c2=7, c3=7, t0=1, t1=1, t2=1, t3=1, t4=1, t5=1,
    x2=3, x3=3, x4=3, h=7, u4=1, u5=3, u6=7, d6=3, f5=1, g6=7, e6=3, lw=3,
)
FIRST = {}
_total = 0
for _name, _count in COUNTS.items():
    FIRST[_name] = _total
    _total += _count
COPIES = _total


def mm(a, b):
    return jnp.dot(a, b, preferred_element_type=f32)


def mm_nt(a, b):
    return lax.dot_general(a, b, (((1,), (1,)), ((), ())), preferred_element_type=f32)


def flip(value, mask):
    out = value
    for bit in range(3):
        if mask >> bit & 1:
            here = lax.rem(lax.div(value, 1 << bit), 2)
            out = out + (1 - 2 * here) * (1 << bit)
    return out


def iota(shape, axis):
    return lax.broadcasted_iota(jnp.int32, shape, axis)


def hot(test):
    return test.astype(f32).astype(bf16)


def kernel(
    rhs_hbm, sep_hbm, inv_hbm, low_hbm, sinv_hbm, slow_hbm, tgt_hbm, live_ref,
    leaf_out, sep_out,
    rhs_ref, sep_ref, inv_ref, low_ref, sinv_ref, slow_ref, tgt_ref, tgs, lsem,
    st, pk, m0, c0, c4, p1, p2, p3, p4, z2, z3, c1, c2, c3, c5, zxs, zxr, eh, dl_, p0, pis, rs_, vs,
    m123, b4, b5, b6, b7, b5o, n5o, n5, n6, n7, i14, i5, i6, hh, u4g, u5g, u6g,
    wq6, wq5, wn6, wn5, e6s, e6r, d6s, d6r, f5s, f5r, g6g, g5v, lws, lwr, lwo, xo, xt, ssem, rsem,
):
    loads = []
    for j, (src, dst) in enumerate((
        (rhs_hbm, rhs_ref), (low_hbm, low_ref), (sep_hbm, sep_ref), (slow_hbm, slow_ref),
        (sinv_hbm, sinv_ref), (tgt_hbm, tgt_ref), (inv_hbm, inv_ref), (tgt_hbm, tgs),
    )):
        loads.append(pltpu.make_async_copy(src, dst, lsem.at[j]))
        loads[-1].start()
    leaf = lax.axis_index("leaf")
    x = lax.axis_index("rhs")
    c = lax.rem(leaf, 2)
    y = lax.rem(lax.div(leaf, 2), 8)
    z = lax.div(leaf, 16)
    dl = lax.rem(leaf, 16)
    zq = lax.rem(z, 4)
    zp = lax.rem(z, 2)
    quad = z - zq
    pair = z - zp

    def dev(zz, yy, cc, xx):
        return (zz * 16 + yy * 2 + cc, xx)

    layer = [(ky, kc) for ky in (4, 3, 5, 2, 6, 7, 1, 0) for kc in (0, 1) if ky or kc]
    barrier = pltpu.get_barrier_semaphore()

    def greet(device):
        pl.semaphore_signal(barrier, inc=1, device_id=device, device_id_type=MESH)

    far = (4, 3, 5, 2, 6, 7, 1)
    for k in far:
        greet(dev(flip(z, k), y, c, x))
        greet(dev(z, flip(y, k), c, x))
        greet(dev(z, flip(y, k), 1 - c, x))
    for k in (2, 1, 3):
        greet(dev(z, y, c, flip(x, k)))
    greet(dev(z, y, 1 - c, x))

    pending = []
    got = {name: [] for name in COUNTS}
    by = {}

    def send(name, src, dst, device, at=None):
        index = FIRST[name] + (len(got[name]) if at is None else at)
        out = pltpu.make_async_remote_copy(
            src_ref=src, dst_ref=dst, send_sem=ssem.at[index], recv_sem=rsem.at[index],
            device_id=device, device_id_type=MESH,
        )
        out.start()
        pending.append(out)
        got[name].append(out)
        by[name, index - FIRST[name]] = out

    def arrive(name):
        for one in got[name]:
            one.wait_recv()

    def scatter(name, buf):
        for k in range(1, 8):
            send(name, buf.at[y, c], buf.at[y, c], dev(z, flip(y, k), c, x))

    def quarter(name, buf):
        for k in range(1, 8):
            send(name, buf.at[y, c, x], buf.at[y, c, x], dev(z, flip(y, k), c, x))

    def planes(name, tag, buf):
        arrive(name)
        for k in range(1, 4):
            send(tag, buf.at[:, c, x], buf.at[:, c, x], dev(z, y, c, flip(x, k)))

    def twin(name, tag, buf):
        arrive(name)
        send(tag, buf.at[:, c], buf.at[:, c], dev(z, y, 1 - c, x))

    def along(name, count, buf, slot):
        for k in far:
            if k < count:
                send(name, buf.at[slot], buf.at[slot], dev(flip(z, k), y, c, x), k - 1)

    loads[0].wait()
    loads[1].wait()
    live = live_ref[0]
    mask = iota((1, 512), 1) < live * 128
    zr = jnp.where(mask, rhs_ref[0], 0.0).astype(bf16)
    zi = jnp.where(mask, rhs_ref[1], 0.0).astype(bf16)
    er = low_ref[0].astype(f32)
    ei = low_ref[1].astype(f32)
    ehv = jnp.concatenate(
        [jnp.concatenate([er, -ei], axis=1), jnp.concatenate([ei, er], axis=1)], axis=0
    ).astype(bf16)
    eh[...] = ehv
    zcat = jnp.concatenate([zr, zi], axis=1)
    st[:, 112:128] = mm_nt(ehv, zcat)
    loads[2].wait()
    for level in range(7):
        st[0:8, 16 * level : 16 * level + 16] = sep_ref[0, level]
        st[8:16, 16 * level : 16 * level + 16] = sep_ref[1, level]
    m0[y, c] = st[...].astype(bf16)
    pk[:, 0:128] = jnp.zeros((16, 128), f32)
    pk[:, 1024:1152] = jnp.zeros((16, 128), f32)
    loads[3].wait()
    loads[4].wait()
    for part in range(2):
        pk[8 * part : 8 * part + 8, 16:1024] = slow_ref[part].astype(f32)
        pk[8 * part : 8 * part + 8, 1040:3072] = sinv_ref[part].astype(f32)
    c0[y, c] = pk[:, 0:256].astype(bf16)
    for t in range(4):
        p4[t] = pk[:, 1024 + 256 * t : 1280 + 256 * t].astype(bf16)
    c4[y, c, x] = p4[x]
    for q in range(4):
        zxs[q, 0] = zr[:, 128 * q : 128 * q + 128]
        zxs[q, 1] = zi[:, 128 * q : 128 * q + 128]
    zxr[x] = zxs[x]
    for t in range(2):
        p1[t] = pk[:, 256 + 128 * t : 384 + 128 * t].astype(bf16)
    for t in range(4):
        p2[t] = pk[:, 512 + 128 * t : 640 + 128 * t].astype(bf16)
    c1[y, c, zp] = p1[zp]
    c5[y, c, zp] = p1[1 - zp]
    z2[zq] = p2[zq]
    loads[5].wait()
    loads[7].wait()
    tgt = tgt_ref[...].astype(f32).astype(bf16)
    spot = iota((128, 1024), 1)
    wide = mm(tgt, hot(iota((128, 1024), 0) == spot // 8))
    place = 8.0 * wide[6:7] + (iota((1, 1024), 1) % 8).astype(f32)
    top_rows = pk[:, 2048:3072].astype(bf16)
    down = iota((1024, 256), 0).astype(f32)
    for t in range(4):
        moved = mm(top_rows, hot(down == place[:, 256 * t : 256 * t + 256])).astype(bf16)
        p3[2 * t] = moved[:, 0:128]
        p3[2 * t + 1] = moved[:, 128:256]
    z3[lax.div(z, 2), zp] = p3[z]

    pl.semaphore_wait(barrier, 25)

    scatter("c0", c0)
    for ky, kc in layer:
        send("msg", m0.at[y, c], m0.at[y, c], dev(z, flip(y, ky), flip(c, kc), x))
    send("q1", p1.at[1 - zp], c1.at[y, c, zp], dev(flip(z, 1), y, c, x))
    for k in range(1, 4):
        send("q2", p2.at[flip(zq, k)], z2.at[zq], dev(flip(z, k), y, c, x))
    for k in range(1, 8):
        send("q3", p3.at[flip(z, k)], z3.at[lax.div(z, 2), zp], dev(flip(z, k), y, c, x))
    quarter("c4", c4)
    send("q0", p1.at[zp], c5.at[y, c, zp], dev(flip(z, 1), y, c, x))
    for k in range(1, 4):
        send("zx", zxs.at[flip(x, k)], zxr.at[x], dev(z, y, c, flip(x, k)))

    lane16 = (iota((1, 256), 1) % 16).astype(f32)
    for s in range(8):
        pick = iota((128, 256), 0) == 16 * s + iota((128, 256), 1) // 16
        dl_[s, 0:7] = 16.0 * mm(tgt, hot(pick)) + lane16
    down = iota((256, 256), 0).astype(f32)

    def route(level, source, slab):
        shift = jnp.asarray(256 * slab, jnp.int32).astype(f32)
        return hot(down + shift == dl_[source][level : level + 1])

    p0[...] = hot(down == dl_[z][0:1] + (iota((1, 256), 1) // 32 * 32).astype(f32))
    lane = iota((1, 256), 1)
    pick = iota((128, 256), 0) == 16 * z + iota((128, 256), 1) % 128 // 8
    inner = (lane // 128 * 8 + lane % 8).astype(f32)
    old = 16.0 * mm(tgt, hot(pick)) + inner
    for level in range(1, 4):
        base = (lane % 128 // 8 // (2 << level) * (2 << level) * 16).astype(f32)
        pis[level - 1] = hot(down == old[level : level + 1] + base)
    rown = iota((256, 1), 0)
    natural = hot(iota((256, 256), 1) == rown % 128 // 8 * 16 + rown // 128 * 8 + rown % 8)
    sign_row = (1 - 2 * (iota((256, 1), 0) // 8 % 2)).astype(f32)
    sign_lane = (1 - 2 * (lane // 8 % 2)).astype(f32)

    def embed(raw):
        parts = raw.reshape(16, 2, 8, 128)
        swapped = jnp.concatenate([parts[:, 1:2], parts[:, 0:1]], axis=1).reshape(256, 128)
        return jnp.concatenate([raw * sign_row, swapped], axis=1).astype(bf16)

    def square(raw):
        return mm(embed(raw.reshape(256, 128).astype(f32)), natural).astype(bf16)

    def small(raw, level):
        size = 8 << level
        at = iota((128, 128), 0)
        to = iota((128, 128), 1)
        repeat = hot(at == size + to % size)
        spread = mm(raw, repeat)
        front = iota((256, 128), 0) // (16 << level) == iota((256, 128), 1) // size
        return embed(jnp.where(front, spread, 0.0))

    def blocks(ref, s):
        return ref[pl.ds(16 * s, 16)].reshape(256, 256)

    arrive("q1")
    scatter("c1", c1)
    twin("c0", "t0", c0)
    arrive("q2")
    c2[y, c, x] = z2[x]
    quarter("c2", c2)
    arrive("q3")
    c3[y, c, x] = z3[x]
    quarter("c3", c3)
    arrive("msg")
    flipped = jnp.transpose(m0[...].reshape(256, 128).astype(f32))
    rs_[...] = flipped
    u = mm_nt(flipped[112:128].astype(bf16), p0[...])
    v = (flipped[0:16] - u).astype(bf16)
    vs[0] = v
    arrive("t0")
    raw0 = c0[:, :, :, 0:128].reshape(256, 128)
    for level in range(1, 4):
        m123[level - 1] = mm_nt(small(raw0, level), pis[level - 1]).astype(bf16)
        u = mm(v, m123[level - 1])
        v = (rs_[16 * level : 16 * level + 16] - u).astype(bf16)
        vs[level] = v
    b4[...] = square(c0[:, :, :, 128:256])
    own = mm(v, b4[...]).astype(bf16)
    u4g[zp] = own
    along("u4", 2, u4g, zp)
    hh[z, 0] = rs_[96:112].astype(bf16)
    hh[z, 1] = rs_[80:96].astype(bf16)
    hh[z, 2] = rs_[64:80].astype(bf16)
    for k in range(1, 8):
        part = pl.ds(0, 3 if k < 2 else 2 if k < 4 else 1)
        send("h", hh.at[z, part], hh.at[z, part], dev(flip(z, k), y, c, x))
    planes("c4", "x4", c4)

    twin("c1", "t1", c1)
    planes("c2", "x2", c2)
    arrive("q0")
    scatter("c5", c5)
    arrive("t1")
    for s in range(2):
        b5[16 * s : 16 * s + 16] = square(c1[:, :, s]).reshape(16, 16, 256)

    def move(level, first, source, target):
        def step(i, carry):
            target[i] = source[tgs[level, first + i]]
            return carry
        return step

    lax.fori_loop(0, 32, move(4, 16 * pair, b5, n5), 0, unroll=8)
    got["h"][0].wait_recv()
    u = -mm(own, blocks(n5, zp))
    for s in range(2):
        u = u + mm(hh[pair + s, 2], blocks(b5, s))
    arrive("u4")
    u = u - mm(u4g[1 - zp], blocks(n5, 1 - zp))
    own = u.astype(bf16)
    u5g[zq] = own
    along("u5", 4, u5g, zq)

    planes("c3", "x3", c3)
    arrive("zx")
    loads[6].wait()
    zr4 = zxr[:, 0].reshape(64, 128)
    zi4 = zxr[:, 1].reshape(64, 128)
    panel = inv_ref[...].reshape(256, 512)
    real = mm(jnp.concatenate([zr4, -zi4], axis=1), panel).reshape(4, 16, 512)
    imag = mm(jnp.concatenate([zi4, zr4], axis=1), panel).reshape(4, 16, 512)
    lwo[:, 0] = real
    lwo[:, 1] = imag
    lws[:, 0] = real.astype(bf16)
    lws[:, 1] = imag.astype(bf16)
    for k in range(1, 4):
        send("lw", lws.at[flip(x, k)], lwr.at[k - 1], dev(z, y, c, flip(x, k)))
    twin("x2", "t2", c2)
    twin("x4", "t4", c4)
    arrive("t2")
    for s in range(4):
        b6[16 * s : 16 * s + 16] = square(c2[:, :, s]).reshape(16, 16, 256)
    lax.fori_loop(0, 64, move(5, 16 * quad, b6, n6), 0, unroll=8)
    got["h"][1].wait_recv()
    got["h"][2].wait_recv()
    u = -mm(own, blocks(n6, zq))
    for s in range(4):
        u = u + mm(hh[quad + s, 1], blocks(b6, s))
    for k in (1, 2, 3):
        by["u5", k - 1].wait_recv()
        u = u - mm(u5g[flip(zq, k)], blocks(n6, flip(zq, k)))
    own = u.astype(bf16)
    u6g[z] = own
    along("u6", 8, u6g, z)

    twin("x3", "t3", c3)
    arrive("t3")
    for s in range(8):
        b7[16 * s : 16 * s + 16] = square(c3[:, :, s // 2, s % 2]).reshape(16, 16, 256)
    lax.fori_loop(0, 128, move(6, 0, b7, n7), 0, unroll=8)
    for k in range(3, 7):
        got["h"][k].wait_recv()
    u = -mm(own, blocks(n7, z))
    for s in range(8):
        u = u + mm(hh[s, 0], blocks(b7, s))

    twin("c5", "t5", c5)
    arrive("t4")
    v5 = rs_[64:80]
    for s in range(2):
        i5[s] = square(c4[:, :, 1, :, 128 * s : 128 * s + 128])
        v5 = v5 - mm_nt(u4g[s], route(4, pair + s, zp))
    v5 = v5.astype(bf16)
    w5 = []
    for s in range(2):
        part = mm(v5, i5[s])
        wn5[s] = part * sign_lane
        w5.append(part.astype(bf16))
    for s in range(2):
        wq5[s] = sign_lane * (
            mm(w5[0], route(4, pair + s, 0)) + mm(w5[1], route(4, pair + s, 1))
        )
    f5s[0] = wq5[1 - zp].astype(bf16)
    f5s[1] = wn5[1 - zp].astype(bf16)
    send("f5", f5s, f5r, dev(flip(z, 1), y, c, x))
    v6 = rs_[80:96]
    for s in range(4):
        i6[s] = square(c4[:, :, 2 + s // 2, :, 128 * (s % 2) : 128 * (s % 2) + 128])
        v6 = v6 - mm_nt(u5g[s], route(5, quad + s, zq))
    v6 = v6.astype(bf16)
    w6 = []
    for s in range(4):
        part = mm(v6, i6[s])
        wn6[s] = part * sign_lane
        w6.append(part.astype(bf16))
    for s in range(4):
        total = mm(w6[0], route(5, quad + s, 0))
        for t in range(1, 4):
            total = total + mm(w6[t], route(5, quad + s, t))
        wq6[s] = total * sign_lane

    for k in (1, 7, 2, 6, 3, 5, 4):
        by["u6", k - 1].wait_recv()
        u = u - mm(u6g[flip(z, k)], blocks(n7, flip(z, k)))
    own = (u * sign_lane).astype(bf16)

    g6g[z] = own
    for k in far[:3]:
        send("g6", g6g.at[z], g6g.at[z], dev(flip(z, k), y, c, x), k - 1)
    half = zq - zp
    for first, targets_k in ((2 - half, (2, 3)), (half, (1,))):
        for j in range(2):
            part = wq6[first + j] - mm_nt(own, blocks(n6, first + j))
            wq6[first + j] = part
            d6s[first + j] = part.astype(bf16)
        for k in targets_k:
            send("d6", d6s.at[pl.ds(first, 2)], d6r.at[k - 1], dev(flip(z, k), y, c, x), k - 1)
    for k in far[3:]:
        send("g6", g6g.at[z], g6g.at[z], dev(flip(z, k), y, c, x), k - 1)
    for k in range(1, 4):
        t = flip(zq, k)
        e6s[k - 1] = (wn6[t] - mm_nt(own, blocks(b6, t))).astype(bf16)
        send("e6", e6s.at[k - 1], e6r.at[k - 1], dev(flip(z, k), y, c, x))
    sixth = wn6[zq] - mm_nt(own, blocks(b6, zq))

    rawi = c4[:, :, 0, :, 0:128].reshape(256, 128)
    for level in range(1, 4):
        i14[level - 1] = mm(small(rawi, level), natural).astype(bf16)
    i14[3] = square(c4[:, :, 0, :, 128:256])
    for level in range(1, 5):
        xo[16 * level - 16 : 16 * level] = mm(vs[level - 1], i14[level - 1]) * sign_lane

    arrive("t5")
    for s in range(2):
        b5o[16 * s : 16 * s + 16] = square(c5[:, :, s]).reshape(16, 16, 256)
    lax.fori_loop(0, 32, move(4, 16 * pair, b5o, n5o), 0, unroll=8)
    arrive("f5")
    parent = wq5[zp] + f5r[0].astype(f32)
    arrive("d6")
    for j in range(2):
        below = wq6[half + j]
        for k in range(3):
            below = below + d6r[k, j].astype(f32)
        g5v[j] = below.astype(bf16)

    def emit(level, size, first, ref):
        want = (16 * (leaf - 16 * first) + iota((16, 256), 0)).astype(f32)
        block = jnp.zeros((16, 16), f32)
        for s in range(size):
            block = block + mm_nt(hot(want == dl_[first + s][level - 1 : level]), ref[s])
        sep_out[0, level - 1] = block[0:8]
        sep_out[1, level - 1] = -block[8:16]

    own = parent - mm_nt(g5v[zp], blocks(n5, zp)) - mm_nt(g5v[1 - zp], blocks(n5o, zp))
    own = own.astype(bf16)
    now = xo[48:64] - mm_nt(own, b4[...])
    xo[48:64] = now
    for level in range(3, 0, -1):
        now = xo[16 * level - 16 : 16 * level] - mm_nt(now.astype(bf16), m123[level - 1])
        xo[16 * level - 16 : 16 * level] = now
    above = 16 * (dl - c + tgs[0, leaf])
    chosen = hot(iota((16, 256), 1) == above + iota((16, 256), 0))
    back = mm_nt(now.astype(bf16), chosen).astype(bf16)
    less = mm(back, eh[...])
    arrive("lw")
    mine = lwo[x]
    for k in range(3):
        mine = mine + lwr[k].astype(f32)
    leaf_out[0] = jnp.where(mask, mine[0] - less[:, 0:512], 0.0)
    leaf_out[1] = jnp.where(mask, mine[1] + less[:, 512:1024], 0.0)

    arrive("e6")
    for k in range(3):
        sixth = sixth + e6r[k].astype(f32)
    xo[64:80] = sixth
    xo[80:96] = (
        wn5[zp] + f5r[1].astype(f32)
        - mm_nt(g5v[zp], blocks(b5, zp)) - mm_nt(g5v[1 - zp], blocks(b5o, zp))
    )
    xo[96:128] = jnp.zeros((32, 256), f32)
    xt[...] = jnp.transpose(xo[...])
    start = pl.multiple_of(dl * 16, 16)
    turned = xt[pl.ds(start, 16), :]
    for row, level in enumerate((0, 1, 2, 3, 5, 4)):
        sep_out[0, level] = turned[0:8, 16 * row : 16 * row + 16]
        sep_out[1, level] = -turned[8:16, 16 * row : 16 * row + 16]
    arrive("g6")
    emit(7, 8, 0, g6g)

    for one in pending:
        one.wait_send()


def body(leaf_rhs, sep_rhs, leaf_inv, leaf_low, sep_inv, sep_low, leaf_live, targets):
    vm = pl.BlockSpec(memory_space=pltpu.VMEM)
    hb = pl.BlockSpec(memory_space=pltpu.HBM)
    sm = pl.BlockSpec(memory_space=pltpu.SMEM)
    V = pltpu.VMEM

    def rows(*lead):
        return V(lead + (16, 256), bf16)

    def squares(count):
        return V((count, 256, 256), bf16)

    out_leaf, out_sep = pl.pallas_call(
        kernel,
        out_shape=(
            jax.ShapeDtypeStruct((2, 16, 512), f32),
            jax.ShapeDtypeStruct((2, 7, 8, 16), f32),
        ),
        in_specs=[hb] * 7 + [sm],
        out_specs=(vm, vm),
        scratch_shapes=[
            V((2, 16, 512), f32), V((2, 7, 8, 16), f32), V((2, 128, 512), bf16),
            V((2, 8, 512), bf16), V((2, 8, 2032), bf16), V((2, 8, 1008), bf16),
            V((7, 128), jnp.int32), pltpu.SMEM((7, 128), jnp.int32),
            pltpu.SemaphoreType.DMA((8,)),
            V((16, 128), f32), V((16, 3072), f32), V((8, 2, 16, 128), bf16),
            V((8, 2, 16, 256), bf16), V((8, 2, 4, 16, 256), bf16),
            V((2, 16, 128), bf16), V((4, 16, 128), bf16), V((8, 16, 128), bf16), rows(4),
            V((4, 16, 128), bf16), V((4, 2, 16, 128), bf16),
            V((8, 2, 2, 16, 128), bf16), V((8, 2, 4, 16, 128), bf16), V((8, 2, 4, 2, 16, 128), bf16), V((8, 2, 2, 16, 128), bf16),
            V((4, 2, 16, 128), bf16), V((4, 2, 16, 128), bf16), V((16, 1024), bf16),
            V((8, 8, 256), f32), V((256, 256), bf16), squares(3),
            V((128, 256), f32), rows(4),
            squares(3), V((256, 256), bf16), rows(32), rows(64), rows(128), rows(32), rows(32),
            rows(32), rows(64), rows(128), squares(4), squares(2), squares(4),
            rows(8, 3), rows(2), rows(4), rows(8),
            V((4, 16, 256), f32), V((2, 16, 256), f32), V((4, 16, 256), f32), V((2, 16, 256), f32), rows(3), rows(3), rows(4), rows(3, 2), rows(2), rows(2),
            rows(8), rows(2),
            V((4, 2, 16, 512), bf16), V((3, 2, 16, 512), bf16), V((4, 2, 16, 512), f32),
            V((128, 256), f32), V((256, 128), f32),
            pltpu.SemaphoreType.DMA((COPIES,)), pltpu.SemaphoreType.DMA((COPIES,)),
        ],
        compiler_params=pltpu.CompilerParams(
            collective_id=0, has_side_effects=True, vmem_limit_bytes=40 * 2**20
        ),
    )(
        *(pltpu.with_memory_space_constraint(one, pltpu.HBM) for one in (
            leaf_rhs, sep_rhs.transpose(0, 2, 3, 1), leaf_inv, leaf_low.transpose(0, 2, 1),
            sep_inv, sep_low, targets,
        )),
        leaf_live,
    )
    return out_leaf, out_sep.transpose(0, 3, 1, 2)


def solution(mesh):
    placed = (
        P(None, "rhs", "leaf"),
        P(None, "rhs", None, "leaf"),
        P(None, "rhs", "leaf"),
        P(None, None, "leaf"),
        P(None, None, "leaf"),
        P(None, None, "leaf"),
        P("leaf"),
        P(),
    )
    return jax.shard_map(
        body,
        mesh=mesh,
        in_specs=placed,
        out_specs=(P(None, "rhs", "leaf"), P(None, "rhs", None, "leaf")),
        check_vma=False,
    )
```

```python
import jax
import jax.numpy as jnp
from jax import lax
from jax.experimental import pallas as pl
from jax.experimental.pallas import tpu as pltpu
from jax.sharding import PartitionSpec as P

MESH = pl.DeviceIdType.MESH
bf16 = jnp.bfloat16
f32 = jnp.float32

COUNTS = dict(
    msg=15, zx=3, c0=7, c4=7, c5=7, q0=1, q1=1, q2=3, q3=7, c1=7, c2=7, c3=7, t0=1, t1=1, t2=1, t3=1, t4=1, t5=1,
    x3=3, x4=3, h=7, u4=1, u5=3, u6=7, d6=3, f5=1, g6=7, e6=3, lw=3,
)
FIRST = {}
_total = 0
for _name, _count in COUNTS.items():
    FIRST[_name] = _total
    _total += _count
COPIES = _total


def mm(a, b):
    return jnp.dot(a, b, preferred_element_type=f32)


def mm_nt(a, b):
    return lax.dot_general(a, b, (((1,), (1,)), ((), ())), preferred_element_type=f32)


def flip(value, mask):
    out = value
    for bit in range(3):
        if mask >> bit & 1:
            here = lax.rem(lax.div(value, 1 << bit), 2)
            out = out + (1 - 2 * here) * (1 << bit)
    return out


def iota(shape, axis):
    return lax.broadcasted_iota(jnp.int32, shape, axis)


def hot(test):
    return test.astype(f32).astype(bf16)


def kernel(
    rhs_hbm, sep_hbm, inv_hbm, low_hbm, sinv_hbm, slow_hbm, tgt_hbm, live_ref,
    leaf_out, sep_out,
    rhs_ref, sep_ref, inv_ref, low_ref, sinv_ref, slow_ref, tgt_ref, tgs, lsem,
    st, pk, m0, c0, c4, p1, p2, p3, p4, z2, z3, c1, c2, c3, c5, zxs, zxr, eh, dl_, p0, pis, rs_, vs,
    m123, b4, b5, b6, b7, b5o, n5o, n5, n6, n7, i14, i5, i6, hh, u4g, u5g, u6g,
    wq6, wq5, wn6, wn5, e6s, e6r, d6s, d6r, f5s, f5r, g6g, g5v, lws, lwr, lwo, xo, xt, ssem, rsem,
):
    loads = []
    for j, (src, dst) in enumerate((
        (rhs_hbm, rhs_ref), (low_hbm, low_ref), (sep_hbm, sep_ref), (slow_hbm, slow_ref),
        (sinv_hbm, sinv_ref), (tgt_hbm, tgt_ref), (inv_hbm, inv_ref), (tgt_hbm, tgs),
    )):
        loads.append(pltpu.make_async_copy(src, dst, lsem.at[j]))
        loads[-1].start()
    leaf = lax.axis_index("leaf")
    x = lax.axis_index("rhs")
    c = lax.rem(leaf, 2)
    y = lax.rem(lax.div(leaf, 2), 8)
    z = lax.div(leaf, 16)
    dl = lax.rem(leaf, 16)
    zq = lax.rem(z, 4)
    zp = lax.rem(z, 2)
    quad = z - zq
    pair = z - zp

    def dev(zz, yy, cc, xx):
        return (zz * 16 + yy * 2 + cc, xx)

    layer = [(ky, kc) for ky in (4, 3, 5, 2, 6, 7, 1, 0) for kc in (0, 1) if ky or kc]
    barrier = pltpu.get_barrier_semaphore()

    def greet(device):
        pl.semaphore_signal(barrier, inc=1, device_id=device, device_id_type=MESH)

    far = (4, 3, 5, 2, 6, 7, 1)
    for k in far:
        greet(dev(flip(z, k), y, c, x))
        greet(dev(z, flip(y, k), c, x))
        greet(dev(z, flip(y, k), 1 - c, x))
    for k in (2, 1, 3):
        greet(dev(z, y, c, flip(x, k)))
    greet(dev(z, y, 1 - c, x))

    pending = []
    got = {name: [] for name in COUNTS}
    by = {}

    def send(name, src, dst, device, at=None):
        index = FIRST[name] + (len(got[name]) if at is None else at)
        out = pltpu.make_async_remote_copy(
            src_ref=src, dst_ref=dst, send_sem=ssem.at[index], recv_sem=rsem.at[index],
            device_id=device, device_id_type=MESH,
        )
        out.start()
        pending.append(out)
        got[name].append(out)
        by[name, index - FIRST[name]] = out

    def arrive(name):
        for one in got[name]:
            one.wait_recv()

    def scatter(name, buf):
        for k in range(1, 8):
            send(name, buf.at[y, c], buf.at[y, c], dev(z, flip(y, k), c, x))

    def quarter(name, buf):
        for k in range(1, 8):
            send(name, buf.at[y, c, x], buf.at[y, c, x], dev(z, flip(y, k), c, x))

    def planes(name, tag, buf):
        arrive(name)
        for k in range(1, 4):
            send(tag, buf.at[:, c, x], buf.at[:, c, x], dev(z, y, c, flip(x, k)))

    def twin(name, tag, buf):
        arrive(name)
        send(tag, buf.at[:, c], buf.at[:, c], dev(z, y, 1 - c, x))

    def along(name, count, buf, slot):
        for k in far:
            if k < count:
                send(name, buf.at[slot], buf.at[slot], dev(flip(z, k), y, c, x), k - 1)

    loads[0].wait()
    loads[1].wait()
    live = live_ref[0]
    mask = iota((1, 512), 1) < live * 128
    zr = jnp.where(mask, rhs_ref[0], 0.0).astype(bf16)
    zi = jnp.where(mask, rhs_ref[1], 0.0).astype(bf16)
    er = low_ref[0].astype(f32)
    ei = low_ref[1].astype(f32)
    ehv = jnp.concatenate(
        [jnp.concatenate([er, -ei], axis=1), jnp.concatenate([ei, er], axis=1)], axis=0
    ).astype(bf16)
    eh[...] = ehv
    zcat = jnp.concatenate([zr, zi], axis=1)
    st[:, 112:128] = mm_nt(ehv, zcat)
    loads[2].wait()
    for level in range(7):
        st[0:8, 16 * level : 16 * level + 16] = sep_ref[0, level]
        st[8:16, 16 * level : 16 * level + 16] = sep_ref[1, level]
    m0[y, c] = st[...].astype(bf16)
    pk[:, 0:128] = jnp.zeros((16, 128), f32)
    pk[:, 1024:1152] = jnp.zeros((16, 128), f32)
    loads[3].wait()
    loads[4].wait()
    for part in range(2):
        pk[8 * part : 8 * part + 8, 16:1024] = slow_ref[part].astype(f32)
        pk[8 * part : 8 * part + 8, 1040:3072] = sinv_ref[part].astype(f32)
    c0[y, c] = pk[:, 0:256].astype(bf16)
    for t in range(4):
        p4[t] = pk[:, 1024 + 256 * t : 1280 + 256 * t].astype(bf16)
    c4[y, c, x] = p4[x]
    for q in range(4):
        zxs[q, 0] = zr[:, 128 * q : 128 * q + 128]
        zxs[q, 1] = zi[:, 128 * q : 128 * q + 128]
    zxr[x] = zxs[x]
    for t in range(2):
        p1[t] = pk[:, 256 + 128 * t : 384 + 128 * t].astype(bf16)
    for t in range(4):
        p2[t] = pk[:, 512 + 128 * t : 640 + 128 * t].astype(bf16)
    c1[y, c, zp] = p1[zp]
    c5[y, c, zp] = p1[1 - zp]
    z2[zq] = p2[zq]
    loads[5].wait()
    loads[7].wait()
    tgt = tgt_ref[...].astype(f32).astype(bf16)
    spot = iota((128, 1024), 1)
    wide = mm(tgt, hot(iota((128, 1024), 0) == spot // 8))
    place = 8.0 * wide[6:7] + (iota((1, 1024), 1) % 8).astype(f32)
    top_rows = pk[:, 2048:3072].astype(bf16)
    down = iota((1024, 256), 0).astype(f32)
    for t in range(4):
        moved = mm(top_rows, hot(down == place[:, 256 * t : 256 * t + 256])).astype(bf16)
        p3[2 * t] = moved[:, 0:128]
        p3[2 * t + 1] = moved[:, 128:256]
    z3[lax.div(z, 2), zp] = p3[z]

    pl.semaphore_wait(barrier, 25)

    for k in far:
        send("q3", p3.at[flip(z, k)], z3.at[lax.div(z, 2), zp], dev(flip(z, k), y, c, x), k - 1)
    scatter("c0", c0)
    for ky, kc in layer:
        send("msg", m0.at[y, c], m0.at[y, c], dev(z, flip(y, ky), flip(c, kc), x))
    send("q1", p1.at[1 - zp], c1.at[y, c, zp], dev(flip(z, 1), y, c, x))
    for k in range(1, 4):
        send("q2", p2.at[flip(zq, k)], z2.at[zq], dev(flip(z, k), y, c, x))
    quarter("c4", c4)
    send("q0", p1.at[zp], c5.at[y, c, zp], dev(flip(z, 1), y, c, x))
    for k in range(1, 4):
        send("zx", zxs.at[flip(x, k)], zxr.at[x], dev(z, y, c, flip(x, k)))

    lane16 = (iota((1, 256), 1) % 16).astype(f32)
    for s in range(8):
        pick = iota((128, 256), 0) == 16 * s + iota((128, 256), 1) // 16
        dl_[s, 0:7] = 16.0 * mm(tgt, hot(pick)) + lane16
    down = iota((256, 256), 0).astype(f32)

    def route(level, source, slab):
        shift = jnp.asarray(256 * slab, jnp.int32).astype(f32)
        return hot(down + shift == dl_[source][level : level + 1])

    p0[...] = hot(down == dl_[z][0:1] + (iota((1, 256), 1) // 32 * 32).astype(f32))
    lane = iota((1, 256), 1)
    pick = iota((128, 256), 0) == 16 * z + iota((128, 256), 1) % 128 // 8
    inner = (lane // 128 * 8 + lane % 8).astype(f32)
    old = 16.0 * mm(tgt, hot(pick)) + inner
    for level in range(1, 4):
        base = (lane % 128 // 8 // (2 << level) * (2 << level) * 16).astype(f32)
        pis[level - 1] = hot(down == old[level : level + 1] + base)
    rown = iota((256, 1), 0)
    natural = hot(iota((256, 256), 1) == rown % 128 // 8 * 16 + rown // 128 * 8 + rown % 8)
    sign_row = (1 - 2 * (iota((256, 1), 0) // 8 % 2)).astype(f32)
    sign_lane = (1 - 2 * (lane // 8 % 2)).astype(f32)

    def embed(raw):
        parts = raw.reshape(16, 2, 8, 128)
        swapped = jnp.concatenate([parts[:, 1:2], parts[:, 0:1]], axis=1).reshape(256, 128)
        return jnp.concatenate([raw * sign_row, swapped], axis=1).astype(bf16)

    def square(raw):
        return mm(embed(raw.reshape(256, 128).astype(f32)), natural).astype(bf16)

    def small(raw, level):
        size = 8 << level
        at = iota((128, 128), 0)
        to = iota((128, 128), 1)
        repeat = hot(at == size + to % size)
        spread = mm(raw, repeat)
        front = iota((256, 128), 0) // (16 << level) == iota((256, 128), 1) // size
        return embed(jnp.where(front, spread, 0.0))

    def blocks(ref, s):
        return ref[pl.ds(16 * s, 16)].reshape(256, 256)

    arrive("q3")
    c3[y, c, x] = z3[x]
    quarter("c3", c3)
    arrive("q1")
    scatter("c1", c1)
    twin("c0", "t0", c0)
    arrive("q2")
    c2[y, c] = z2[...]
    scatter("c2", c2)
    arrive("msg")
    flipped = jnp.transpose(m0[...].reshape(256, 128).astype(f32))
    rs_[...] = flipped
    u = mm_nt(flipped[112:128].astype(bf16), p0[...])
    v = (flipped[0:16] - u).astype(bf16)
    vs[0] = v
    arrive("t0")
    raw0 = c0[:, :, :, 0:128].reshape(256, 128)
    for level in range(1, 4):
        m123[level - 1] = mm_nt(small(raw0, level), pis[level - 1]).astype(bf16)
        u = mm(v, m123[level - 1])
        v = (rs_[16 * level : 16 * level + 16] - u).astype(bf16)
        vs[level] = v
    b4[...] = square(c0[:, :, :, 128:256])
    own = mm(v, b4[...]).astype(bf16)
    u4g[zp] = own
    along("u4", 2, u4g, zp)
    hh[z, 0] = rs_[96:112].astype(bf16)
    hh[z, 1] = rs_[80:96].astype(bf16)
    hh[z, 2] = rs_[64:80].astype(bf16)
    for k in range(1, 8):
        part = pl.ds(0, 3 if k < 2 else 2 if k < 4 else 1)
        send("h", hh.at[z, part], hh.at[z, part], dev(flip(z, k), y, c, x))
    planes("c4", "x4", c4)

    twin("c1", "t1", c1)
    arrive("q0")
    scatter("c5", c5)
    arrive("t1")
    for s in range(2):
        b5[16 * s : 16 * s + 16] = square(c1[:, :, s]).reshape(16, 16, 256)

    def move(level, first, source, target):
        def step(i, carry):
            target[i] = source[tgs[level, first + i]]
            return carry
        return step

    lax.fori_loop(0, 32, move(4, 16 * pair, b5, n5), 0, unroll=8)
    got["h"][0].wait_recv()
    u = -mm(own, blocks(n5, zp))
    for s in range(2):
        u = u + mm(hh[pair + s, 2], blocks(b5, s))
    planes("c3", "x3", c3)
    arrive("u4")
    u = u - mm(u4g[1 - zp], blocks(n5, 1 - zp))
    own = u.astype(bf16)
    u5g[zq] = own
    along("u5", 4, u5g, zq)

    arrive("zx")
    loads[6].wait()
    zr4 = zxr[:, 0].reshape(64, 128)
    zi4 = zxr[:, 1].reshape(64, 128)
    panel = inv_ref[...].reshape(256, 512)
    real = mm(jnp.concatenate([zr4, -zi4], axis=1), panel).reshape(4, 16, 512)
    imag = mm(jnp.concatenate([zi4, zr4], axis=1), panel).reshape(4, 16, 512)
    lwo[:, 0] = real
    lwo[:, 1] = imag
    lws[:, 0] = real.astype(bf16)
    lws[:, 1] = imag.astype(bf16)
    for k in range(1, 4):
        send("lw", lws.at[flip(x, k)], lwr.at[k - 1], dev(z, y, c, flip(x, k)))
    twin("c2", "t2", c2)
    arrive("t2")
    for s in range(4):
        b6[16 * s : 16 * s + 16] = square(c2[:, :, s]).reshape(16, 16, 256)
    lax.fori_loop(0, 64, move(5, 16 * quad, b6, n6), 0, unroll=8)
    got["h"][1].wait_recv()
    got["h"][2].wait_recv()
    u = -mm(own, blocks(n6, zq))
    for s in range(4):
        u = u + mm(hh[quad + s, 1], blocks(b6, s))
    for k in (1, 2, 3):
        by["u5", k - 1].wait_recv()
        u = u - mm(u5g[flip(zq, k)], blocks(n6, flip(zq, k)))
    own = u.astype(bf16)
    u6g[z] = own
    along("u6", 8, u6g, z)
    twin("x4", "t4", c4)

    arrive("t4")
    v5 = rs_[64:80]
    for s in range(2):
        i5[s] = square(c4[:, :, 1, :, 128 * s : 128 * s + 128])
        v5 = v5 - mm_nt(u4g[s], route(4, pair + s, zp))
    v5 = v5.astype(bf16)
    w5 = []
    for s in range(2):
        part = mm(v5, i5[s])
        wn5[s] = part * sign_lane
        w5.append(part.astype(bf16))
    for s in range(2):
        wq5[s] = sign_lane * (
            mm(w5[0], route(4, pair + s, 0)) + mm(w5[1], route(4, pair + s, 1))
        )
    f5s[0] = wq5[1 - zp].astype(bf16)
    f5s[1] = wn5[1 - zp].astype(bf16)
    send("f5", f5s, f5r, dev(flip(z, 1), y, c, x))
    v6 = rs_[80:96]
    for s in range(4):
        i6[s] = square(c4[:, :, 2 + s // 2, :, 128 * (s % 2) : 128 * (s % 2) + 128])
        v6 = v6 - mm_nt(u5g[s], route(5, quad + s, zq))
    v6 = v6.astype(bf16)
    w6 = []
    for s in range(4):
        part = mm(v6, i6[s])
        wn6[s] = part * sign_lane
        w6.append(part.astype(bf16))
    for s in range(4):
        total = mm(w6[0], route(5, quad + s, 0))
        for t in range(1, 4):
            total = total + mm(w6[t], route(5, quad + s, t))
        wq6[s] = total * sign_lane

    twin("x3", "t3", c3)
    twin("c5", "t5", c5)
    arrive("t3")
    for s in range(8):
        b7[16 * s : 16 * s + 16] = square(c3[:, :, s // 2, s % 2]).reshape(16, 16, 256)
    lax.fori_loop(0, 128, move(6, 0, b7, n7), 0, unroll=8)
    for k in range(3, 7):
        got["h"][k].wait_recv()
    u = -mm(own, blocks(n7, z))
    for s in range(8):
        u = u + mm(hh[s, 0], blocks(b7, s))

    for k in (1, 7, 2, 6, 3, 5, 4):
        by["u6", k - 1].wait_recv()
        u = u - mm(u6g[flip(z, k)], blocks(n7, flip(z, k)))
    own = (u * sign_lane).astype(bf16)

    g6g[z] = own
    for k in far[:3]:
        send("g6", g6g.at[z], g6g.at[z], dev(flip(z, k), y, c, x), k - 1)
    half = zq - zp
    for first, targets_k in ((2 - half, (2, 3)), (half, (1,))):
        for j in range(2):
            part = wq6[first + j] - mm_nt(own, blocks(n6, first + j))
            wq6[first + j] = part
            d6s[first + j] = part.astype(bf16)
        for k in targets_k:
            send("d6", d6s.at[pl.ds(first, 2)], d6r.at[k - 1], dev(flip(z, k), y, c, x), k - 1)
    for k in far[3:]:
        send("g6", g6g.at[z], g6g.at[z], dev(flip(z, k), y, c, x), k - 1)
    for k in range(1, 4):
        t = flip(zq, k)
        e6s[k - 1] = (wn6[t] - mm_nt(own, blocks(b6, t))).astype(bf16)
        send("e6", e6s.at[k - 1], e6r.at[k - 1], dev(flip(z, k), y, c, x))
    sixth = wn6[zq] - mm_nt(own, blocks(b6, zq))

    rawi = c4[:, :, 0, :, 0:128].reshape(256, 128)
    for level in range(1, 4):
        i14[level - 1] = mm(small(rawi, level), natural).astype(bf16)
    i14[3] = square(c4[:, :, 0, :, 128:256])
    for level in range(1, 5):
        xo[16 * level - 16 : 16 * level] = mm(vs[level - 1], i14[level - 1]) * sign_lane

    arrive("t5")
    for s in range(2):
        b5o[16 * s : 16 * s + 16] = square(c5[:, :, s]).reshape(16, 16, 256)
    lax.fori_loop(0, 32, move(4, 16 * pair, b5o, n5o), 0, unroll=8)
    arrive("f5")
    parent = wq5[zp] + f5r[0].astype(f32)
    arrive("d6")
    for j in range(2):
        below = wq6[half + j]
        for k in range(3):
            below = below + d6r[k, j].astype(f32)
        g5v[j] = below.astype(bf16)

    def emit(level, size, first, ref):
        want = (16 * (leaf - 16 * first) + iota((16, 256), 0)).astype(f32)
        block = jnp.zeros((16, 16), f32)
        for s in range(size):
            block = block + mm_nt(hot(want == dl_[first + s][level - 1 : level]), ref[s])
        sep_out[0, level - 1] = block[0:8]
        sep_out[1, level - 1] = -block[8:16]

    own = parent - mm_nt(g5v[zp], blocks(n5, zp)) - mm_nt(g5v[1 - zp], blocks(n5o, zp))
    own = own.astype(bf16)
    now = xo[48:64] - mm_nt(own, b4[...])
    xo[48:64] = now
    for level in range(3, 0, -1):
        now = xo[16 * level - 16 : 16 * level] - mm_nt(now.astype(bf16), m123[level - 1])
        xo[16 * level - 16 : 16 * level] = now
    above = 16 * (dl - c + tgs[0, leaf])
    chosen = hot(iota((16, 256), 1) == above + iota((16, 256), 0))
    back = mm_nt(now.astype(bf16), chosen).astype(bf16)
    less = mm(back, eh[...])
    arrive("lw")
    mine = lwo[x]
    for k in range(3):
        mine = mine + lwr[k].astype(f32)
    leaf_out[0] = jnp.where(mask, mine[0] - less[:, 0:512], 0.0)
    leaf_out[1] = jnp.where(mask, mine[1] + less[:, 512:1024], 0.0)

    arrive("e6")
    for k in range(3):
        sixth = sixth + e6r[k].astype(f32)
    xo[64:80] = sixth
    xo[80:96] = (
        wn5[zp] + f5r[1].astype(f32)
        - mm_nt(g5v[zp], blocks(b5, zp)) - mm_nt(g5v[1 - zp], blocks(b5o, zp))
    )
    xo[96:128] = jnp.zeros((32, 256), f32)
    xt[...] = jnp.transpose(xo[...])
    start = pl.multiple_of(dl * 16, 16)
    turned = xt[pl.ds(start, 16), :]
    for row, level in enumerate((0, 1, 2, 3, 5, 4)):
        sep_out[0, level] = turned[0:8, 16 * row : 16 * row + 16]
        sep_out[1, level] = -turned[8:16, 16 * row : 16 * row + 16]
    arrive("g6")
    emit(7, 8, 0, g6g)

    for one in pending:
        one.wait_send()


def body(leaf_rhs, sep_rhs, leaf_inv, leaf_low, sep_inv, sep_low, leaf_live, targets):
    vm = pl.BlockSpec(memory_space=pltpu.VMEM)
    hb = pl.BlockSpec(memory_space=pltpu.HBM)
    sm = pl.BlockSpec(memory_space=pltpu.SMEM)
    V = pltpu.VMEM

    def rows(*lead):
        return V(lead + (16, 256), bf16)

    def squares(count):
        return V((count, 256, 256), bf16)

    out_leaf, out_sep = pl.pallas_call(
        kernel,
        out_shape=(
            jax.ShapeDtypeStruct((2, 16, 512), f32),
            jax.ShapeDtypeStruct((2, 7, 8, 16), f32),
        ),
        in_specs=[hb] * 7 + [sm],
        out_specs=(vm, vm),
        scratch_shapes=[
            V((2, 16, 512), f32), V((2, 7, 8, 16), f32), V((2, 128, 512), bf16),
            V((2, 8, 512), bf16), V((2, 8, 2032), bf16), V((2, 8, 1008), bf16),
            V((7, 128), jnp.int32), pltpu.SMEM((7, 128), jnp.int32),
            pltpu.SemaphoreType.DMA((8,)),
            V((16, 128), f32), V((16, 3072), f32), V((8, 2, 16, 128), bf16),
            V((8, 2, 16, 256), bf16), V((8, 2, 4, 16, 256), bf16),
            V((2, 16, 128), bf16), V((4, 16, 128), bf16), V((8, 16, 128), bf16), rows(4),
            V((4, 16, 128), bf16), V((4, 2, 16, 128), bf16),
            V((8, 2, 2, 16, 128), bf16), V((8, 2, 4, 16, 128), bf16), V((8, 2, 4, 2, 16, 128), bf16), V((8, 2, 2, 16, 128), bf16),
            V((4, 2, 16, 128), bf16), V((4, 2, 16, 128), bf16), V((16, 1024), bf16),
            V((8, 8, 256), f32), V((256, 256), bf16), squares(3),
            V((128, 256), f32), rows(4),
            squares(3), V((256, 256), bf16), rows(32), rows(64), rows(128), rows(32), rows(32),
            rows(32), rows(64), rows(128), squares(4), squares(2), squares(4),
            rows(8, 3), rows(2), rows(4), rows(8),
            V((4, 16, 256), f32), V((2, 16, 256), f32), V((4, 16, 256), f32), V((2, 16, 256), f32), rows(3), rows(3), rows(4), rows(3, 2), rows(2), rows(2),
            rows(8), rows(2),
            V((4, 2, 16, 512), bf16), V((3, 2, 16, 512), bf16), V((4, 2, 16, 512), f32),
            V((128, 256), f32), V((256, 128), f32),
            pltpu.SemaphoreType.DMA((COPIES,)), pltpu.SemaphoreType.DMA((COPIES,)),
        ],
        compiler_params=pltpu.CompilerParams(
            collective_id=0, has_side_effects=True, vmem_limit_bytes=40 * 2**20
        ),
    )(
        *(pltpu.with_memory_space_constraint(one, pltpu.HBM) for one in (
            leaf_rhs, sep_rhs.transpose(0, 2, 3, 1), leaf_inv, leaf_low.transpose(0, 2, 1),
            sep_inv, sep_low, targets,
        )),
        leaf_live,
    )
    return out_leaf, out_sep.transpose(0, 3, 1, 2)


def solution(mesh):
    placed = (
        P(None, "rhs", "leaf"),
        P(None, "rhs", None, "leaf"),
        P(None, "rhs", "leaf"),
        P(None, None, "leaf"),
        P(None, None, "leaf"),
        P(None, None, "leaf"),
        P("leaf"),
        P(),
    )
    return jax.shard_map(
        body,
        mesh=mesh,
        in_specs=placed,
        out_specs=(P(None, "rhs", "leaf"), P(None, "rhs", None, "leaf")),
        check_vma=False,
    )
```

```python
import jax
import jax.numpy as jnp
from jax import lax
from jax.experimental import pallas as pl
from jax.experimental.pallas import tpu as pltpu
from jax.sharding import PartitionSpec as P

MESH = pl.DeviceIdType.MESH
bf16 = jnp.bfloat16
f32 = jnp.float32

COUNTS = dict(
    msg=15, zx=3, c0=7, c4=7, c5=7, q0=1, q1=1, q2=3, q3=7, c1=7, c2=7, c3=7, t0=1, t1=1, t2=1, t3=1, t4=1, t5=1,
    x3=3, x4=3, h=7, u4=1, u5=3, u6=7, d6=3, f5=1, g6=7, e6=3, lw=3,
)
FIRST = {}
_total = 0
for _name, _count in COUNTS.items():
    FIRST[_name] = _total
    _total += _count
COPIES = _total


def mm(a, b):
    return jnp.dot(a, b, preferred_element_type=f32)


def mm_nt(a, b):
    return lax.dot_general(a, b, (((1,), (1,)), ((), ())), preferred_element_type=f32)


def flip(value, mask):
    out = value
    for bit in range(3):
        if mask >> bit & 1:
            here = lax.rem(lax.div(value, 1 << bit), 2)
            out = out + (1 - 2 * here) * (1 << bit)
    return out


def iota(shape, axis):
    return lax.broadcasted_iota(jnp.int32, shape, axis)


def hot(test):
    return test.astype(f32).astype(bf16)


def kernel(
    rhs_hbm, sep_hbm, inv_hbm, low_hbm, sinv_hbm, slow_hbm, tgt_hbm, live_ref,
    leaf_out, sep_out,
    rhs_ref, sep_ref, inv_ref, low_ref, sinv_ref, slow_ref, tgt_ref, tgs, lsem,
    st, pk, m0, c0, c4, p1, p2, p3, p4, z2, z3, c1, c2, c3, c5, zxs, zxr, eh, dl_, p0, pis, rs_, vs,
    m123, b4, b5, b6, b7, b5o, n5o, n5, n6, n7, i14, i5, i6, hh, u4g, u5g, u6g,
    wq6, wq5, wn6, wn5, e6s, e6r, d6s, d6r, f5s, f5r, g6g, g5v, lws, lwr, lwo, xo, xt, ssem, rsem,
):
    loads = []
    for j, (src, dst) in enumerate((
        (rhs_hbm, rhs_ref), (low_hbm, low_ref), (sep_hbm, sep_ref), (slow_hbm, slow_ref),
        (sinv_hbm, sinv_ref), (tgt_hbm, tgt_ref), (inv_hbm, inv_ref), (tgt_hbm, tgs),
    )):
        loads.append(pltpu.make_async_copy(src, dst, lsem.at[j]))
        loads[-1].start()
    leaf = lax.axis_index("leaf")
    x = lax.axis_index("rhs")
    c = lax.rem(leaf, 2)
    y = lax.rem(lax.div(leaf, 2), 8)
    z = lax.div(leaf, 16)
    dl = lax.rem(leaf, 16)
    zq = lax.rem(z, 4)
    zp = lax.rem(z, 2)
    quad = z - zq
    pair = z - zp

    def dev(zz, yy, cc, xx):
        return (zz * 16 + yy * 2 + cc, xx)

    layer = [(ky, kc) for ky in (4, 3, 5, 2, 6, 7, 1, 0) for kc in (0, 1) if ky or kc]
    barrier = pltpu.get_barrier_semaphore()

    def greet(device):
        pl.semaphore_signal(barrier, inc=1, device_id=device, device_id_type=MESH)

    far = (4, 3, 5, 2, 6, 7, 1)
    for k in far:
        greet(dev(flip(z, k), y, c, x))
        greet(dev(z, flip(y, k), c, x))
        greet(dev(z, flip(y, k), 1 - c, x))
    for k in (2, 1, 3):
        greet(dev(z, y, c, flip(x, k)))
    greet(dev(z, y, 1 - c, x))

    pending = []
    got = {name: [] for name in COUNTS}
    by = {}

    def send(name, src, dst, device, at=None):
        index = FIRST[name] + (len(got[name]) if at is None else at)
        out = pltpu.make_async_remote_copy(
            src_ref=src, dst_ref=dst, send_sem=ssem.at[index], recv_sem=rsem.at[index],
            device_id=device, device_id_type=MESH,
        )
        out.start()
        pending.append(out)
        got[name].append(out)
        by[name, index - FIRST[name]] = out

    def arrive(name):
        for one in got[name]:
            one.wait_recv()

    def scatter(name, buf):
        for k in range(1, 8):
            send(name, buf.at[y, c], buf.at[y, c], dev(z, flip(y, k), c, x))

    def quarter(name, buf):
        for k in range(1, 8):
            send(name, buf.at[y, c, x], buf.at[y, c, x], dev(z, flip(y, k), c, x))

    def planes(name, tag, buf):
        arrive(name)
        for k in range(1, 4):
            send(tag, buf.at[:, c, x], buf.at[:, c, x], dev(z, y, c, flip(x, k)))

    def twin(name, tag, buf):
        arrive(name)
        send(tag, buf.at[:, c], buf.at[:, c], dev(z, y, 1 - c, x))

    def along(name, count, buf, slot):
        for k in far:
            if k < count:
                send(name, buf.at[slot], buf.at[slot], dev(flip(z, k), y, c, x), k - 1)

    loads[0].wait()
    loads[1].wait()
    live = live_ref[0]
    mask = iota((1, 512), 1) < live * 128
    zr = jnp.where(mask, rhs_ref[0], 0.0).astype(bf16)
    zi = jnp.where(mask, rhs_ref[1], 0.0).astype(bf16)
    er = low_ref[0].astype(f32)
    ei = low_ref[1].astype(f32)
    ehv = jnp.concatenate(
        [jnp.concatenate([er, -ei], axis=1), jnp.concatenate([ei, er], axis=1)], axis=0
    ).astype(bf16)
    eh[...] = ehv
    zcat = jnp.concatenate([zr, zi], axis=1)
    st[:, 112:128] = mm_nt(ehv, zcat)
    loads[2].wait()
    for level in range(7):
        st[0:8, 16 * level : 16 * level + 16] = sep_ref[0, level]
        st[8:16, 16 * level : 16 * level + 16] = sep_ref[1, level]
    m0[y, c] = st[...].astype(bf16)
    pk[:, 0:128] = jnp.zeros((16, 128), f32)
    pk[:, 1024:1152] = jnp.zeros((16, 128), f32)
    loads[3].wait()
    loads[4].wait()
    for part in range(2):
        pk[8 * part : 8 * part + 8, 16:1024] = slow_ref[part].astype(f32)
        pk[8 * part : 8 * part + 8, 1040:3072] = sinv_ref[part].astype(f32)
    c0[y, c] = pk[:, 0:256].astype(bf16)
    for t in range(4):
        p4[t] = pk[:, 1024 + 256 * t : 1280 + 256 * t].astype(bf16)
    c4[y, c, x] = p4[x]
    for q in range(4):
        zxs[q, 0] = zr[:, 128 * q : 128 * q + 128]
        zxs[q, 1] = zi[:, 128 * q : 128 * q + 128]
    zxr[x] = zxs[x]
    for t in range(2):
        p1[t] = pk[:, 256 + 128 * t : 384 + 128 * t].astype(bf16)
    for t in range(4):
        p2[t] = pk[:, 512 + 128 * t : 640 + 128 * t].astype(bf16)
    c1[y, c, zp] = p1[zp]
    c5[y, c, zp] = p1[1 - zp]
    z2[zq] = p2[zq]
    loads[5].wait()
    loads[7].wait()
    tgt = tgt_ref[...].astype(f32).astype(bf16)
    spot = iota((128, 1024), 1)
    wide = mm(tgt, hot(iota((128, 1024), 0) == spot // 8))
    place = 8.0 * wide[6:7] + (iota((1, 1024), 1) % 8).astype(f32)
    top_rows = pk[:, 2048:3072].astype(bf16)
    down = iota((1024, 256), 0).astype(f32)
    for t in range(4):
        moved = mm(top_rows, hot(down == place[:, 256 * t : 256 * t + 256])).astype(bf16)
        p3[2 * t] = moved[:, 0:128]
        p3[2 * t + 1] = moved[:, 128:256]
    z3[lax.div(z, 2), zp] = p3[z]

    pl.semaphore_wait(barrier, 25)

    for k in far:
        send("q3", p3.at[flip(z, k)], z3.at[lax.div(z, 2), zp], dev(flip(z, k), y, c, x), k - 1)
    for ky, kc in layer:
        send("msg", m0.at[y, c], m0.at[y, c], dev(z, flip(y, ky), flip(c, kc), x))
    scatter("c0", c0)
    send("q1", p1.at[1 - zp], c1.at[y, c, zp], dev(flip(z, 1), y, c, x))
    for k in range(1, 4):
        send("q2", p2.at[flip(zq, k)], z2.at[zq], dev(flip(z, k), y, c, x))
    quarter("c4", c4)
    send("q0", p1.at[zp], c5.at[y, c, zp], dev(flip(z, 1), y, c, x))
    for k in range(1, 4):
        send("zx", zxs.at[flip(x, k)], zxr.at[x], dev(z, y, c, flip(x, k)))

    lane16 = (iota((1, 256), 1) % 16).astype(f32)
    for s in range(8):
        pick = iota((128, 256), 0) == 16 * s + iota((128, 256), 1) // 16
        dl_[s, 0:7] = 16.0 * mm(tgt, hot(pick)) + lane16
    down = iota((256, 256), 0).astype(f32)

    def route(level, source, slab):
        shift = jnp.asarray(256 * slab, jnp.int32).astype(f32)
        return hot(down + shift == dl_[source][level : level + 1])

    p0[...] = hot(down == dl_[z][0:1] + (iota((1, 256), 1) // 32 * 32).astype(f32))
    lane = iota((1, 256), 1)
    pick = iota((128, 256), 0) == 16 * z + iota((128, 256), 1) % 128 // 8
    inner = (lane // 128 * 8 + lane % 8).astype(f32)
    old = 16.0 * mm(tgt, hot(pick)) + inner
    for level in range(1, 4):
        base = (lane % 128 // 8 // (2 << level) * (2 << level) * 16).astype(f32)
        pis[level - 1] = hot(down == old[level : level + 1] + base)
    rown = iota((256, 1), 0)
    natural = hot(iota((256, 256), 1) == rown % 128 // 8 * 16 + rown // 128 * 8 + rown % 8)
    sign_row = (1 - 2 * (iota((256, 1), 0) // 8 % 2)).astype(f32)
    sign_lane = (1 - 2 * (lane // 8 % 2)).astype(f32)

    def embed(raw):
        parts = raw.reshape(16, 2, 8, 128)
        swapped = jnp.concatenate([parts[:, 1:2], parts[:, 0:1]], axis=1).reshape(256, 128)
        return jnp.concatenate([raw * sign_row, swapped], axis=1).astype(bf16)

    def square(raw):
        return mm(embed(raw.reshape(256, 128).astype(f32)), natural).astype(bf16)

    def small(raw, level):
        size = 8 << level
        at = iota((128, 128), 0)
        to = iota((128, 128), 1)
        repeat = hot(at == size + to % size)
        spread = mm(raw, repeat)
        front = iota((256, 128), 0) // (16 << level) == iota((256, 128), 1) // size
        return embed(jnp.where(front, spread, 0.0))

    def blocks(ref, s):
        return ref[pl.ds(16 * s, 16)].reshape(256, 256)

    arrive("q3")
    c3[y, c, x] = z3[x]
    quarter("c3", c3)
    arrive("q1")
    scatter("c1", c1)
    twin("c0", "t0", c0)
    arrive("q2")
    c2[y, c] = z2[...]
    scatter("c2", c2)
    arrive("msg")
    flipped = jnp.transpose(m0[...].reshape(256, 128).astype(f32))
    rs_[...] = flipped
    u = mm_nt(flipped[112:128].astype(bf16), p0[...])
    v = (flipped[0:16] - u).astype(bf16)
    vs[0] = v
    arrive("t0")
    raw0 = c0[:, :, :, 0:128].reshape(256, 128)
    for level in range(1, 4):
        m123[level - 1] = mm_nt(small(raw0, level), pis[level - 1]).astype(bf16)
        u = mm(v, m123[level - 1])
        v = (rs_[16 * level : 16 * level + 16] - u).astype(bf16)
        vs[level] = v
    b4[...] = square(c0[:, :, :, 128:256])
    own = mm(v, b4[...]).astype(bf16)
    u4g[zp] = own
    along("u4", 2, u4g, zp)
    hh[z, 0] = rs_[96:112].astype(bf16)
    hh[z, 1] = rs_[80:96].astype(bf16)
    hh[z, 2] = rs_[64:80].astype(bf16)
    for k in range(1, 8):
        part = pl.ds(0, 3 if k < 2 else 2 if k < 4 else 1)
        send("h", hh.at[z, part], hh.at[z, part], dev(flip(z, k), y, c, x))
    planes("c4", "x4", c4)

    twin("c1", "t1", c1)
    arrive("q0")
    scatter("c5", c5)
    arrive("t1")
    for s in range(2):
        b5[16 * s : 16 * s + 16] = square(c1[:, :, s]).reshape(16, 16, 256)

    def move(level, first, source, target):
        def step(i, carry):
            target[i] = source[tgs[level, first + i]]
            return carry
        return step

    lax.fori_loop(0, 32, move(4, 16 * pair, b5, n5), 0, unroll=8)
    got["h"][0].wait_recv()
    u = -mm(own, blocks(n5, zp))
    for s in range(2):
        u = u + mm(hh[pair + s, 2], blocks(b5, s))
    planes("c3", "x3", c3)
    arrive("u4")
    u = u - mm(u4g[1 - zp], blocks(n5, 1 - zp))
    own = u.astype(bf16)
    u5g[zq] = own
    along("u5", 4, u5g, zq)

    arrive("zx")
    loads[6].wait()
    zr4 = zxr[:, 0].reshape(64, 128)
    zi4 = zxr[:, 1].reshape(64, 128)
    panel = inv_ref[...].reshape(256, 512)
    real = mm(jnp.concatenate([zr4, -zi4], axis=1), panel).reshape(4, 16, 512)
    imag = mm(jnp.concatenate([zi4, zr4], axis=1), panel).reshape(4, 16, 512)
    lwo[:, 0] = real
    lwo[:, 1] = imag
    lws[:, 0] = real.astype(bf16)
    lws[:, 1] = imag.astype(bf16)
    for k in range(1, 4):
        send("lw", lws.at[flip(x, k)], lwr.at[k - 1], dev(z, y, c, flip(x, k)))
    twin("c2", "t2", c2)
    arrive("t2")
    for s in range(4):
        b6[16 * s : 16 * s + 16] = square(c2[:, :, s]).reshape(16, 16, 256)
    lax.fori_loop(0, 64, move(5, 16 * quad, b6, n6), 0, unroll=8)
    got["h"][1].wait_recv()
    got["h"][2].wait_recv()
    u = -mm(own, blocks(n6, zq))
    for s in range(4):
        u = u + mm(hh[quad + s, 1], blocks(b6, s))
    for k in (1, 2, 3):
        by["u5", k - 1].wait_recv()
        u = u - mm(u5g[flip(zq, k)], blocks(n6, flip(zq, k)))
    own = u.astype(bf16)
    u6g[z] = own
    along("u6", 8, u6g, z)
    twin("x4", "t4", c4)

    arrive("t4")
    v5 = rs_[64:80]
    for s in range(2):
        i5[s] = square(c4[:, :, 1, :, 128 * s : 128 * s + 128])
        v5 = v5 - mm_nt(u4g[s], route(4, pair + s, zp))
    v5 = v5.astype(bf16)
    w5 = []
    for s in range(2):
        part = mm(v5, i5[s])
        wn5[s] = part * sign_lane
        w5.append(part.astype(bf16))
    for s in range(2):
        wq5[s] = sign_lane * (
            mm(w5[0], route(4, pair + s, 0)) + mm(w5[1], route(4, pair + s, 1))
        )
    f5s[0] = wq5[1 - zp].astype(bf16)
    f5s[1] = wn5[1 - zp].astype(bf16)
    send("f5", f5s, f5r, dev(flip(z, 1), y, c, x))
    v6 = rs_[80:96]
    for s in range(4):
        i6[s] = square(c4[:, :, 2 + s // 2, :, 128 * (s % 2) : 128 * (s % 2) + 128])
        v6 = v6 - mm_nt(u5g[s], route(5, quad + s, zq))
    v6 = v6.astype(bf16)
    w6 = []
    for s in range(4):
        part = mm(v6, i6[s])
        wn6[s] = part * sign_lane
        w6.append(part.astype(bf16))
    for s in range(4):
        total = mm(w6[0], route(5, quad + s, 0))
        for t in range(1, 4):
            total = total + mm(w6[t], route(5, quad + s, t))
        wq6[s] = total * sign_lane

    twin("x3", "t3", c3)
    twin("c5", "t5", c5)
    arrive("t3")
    for s in range(8):
        b7[16 * s : 16 * s + 16] = square(c3[:, :, s // 2, s % 2]).reshape(16, 16, 256)
    lax.fori_loop(0, 128, move(6, 0, b7, n7), 0, unroll=8)
    for k in range(3, 7):
        got["h"][k].wait_recv()
    u = -mm(own, blocks(n7, z))
    for s in range(8):
        u = u + mm(hh[s, 0], blocks(b7, s))

    for k in (1, 7, 2, 6, 3, 5, 4):
        by["u6", k - 1].wait_recv()
        u = u - mm(u6g[flip(z, k)], blocks(n7, flip(z, k)))
    own = (u * sign_lane).astype(bf16)

    g6g[z] = own
    for k in far[:3]:
        send("g6", g6g.at[z], g6g.at[z], dev(flip(z, k), y, c, x), k - 1)
    half = zq - zp
    for first, targets_k in ((2 - half, (2, 3)), (half, (1,))):
        for j in range(2):
            part = wq6[first + j] - mm_nt(own, blocks(n6, first + j))
            wq6[first + j] = part
            d6s[first + j] = part.astype(bf16)
        for k in targets_k:
            send("d6", d6s.at[pl.ds(first, 2)], d6r.at[k - 1], dev(flip(z, k), y, c, x), k - 1)
    for k in far[3:]:
        send("g6", g6g.at[z], g6g.at[z], dev(flip(z, k), y, c, x), k - 1)
    for k in range(1, 4):
        t = flip(zq, k)
        e6s[k - 1] = (wn6[t] - mm_nt(own, blocks(b6, t))).astype(bf16)
        send("e6", e6s.at[k - 1], e6r.at[k - 1], dev(flip(z, k), y, c, x))
    sixth = wn6[zq] - mm_nt(own, blocks(b6, zq))

    rawi = c4[:, :, 0, :, 0:128].reshape(256, 128)
    for level in range(1, 4):
        i14[level - 1] = mm(small(rawi, level), natural).astype(bf16)
    i14[3] = square(c4[:, :, 0, :, 128:256])
    for level in range(1, 5):
        xo[16 * level - 16 : 16 * level] = mm(vs[level - 1], i14[level - 1]) * sign_lane

    arrive("t5")
    for s in range(2):
        b5o[16 * s : 16 * s + 16] = square(c5[:, :, s]).reshape(16, 16, 256)
    lax.fori_loop(0, 32, move(4, 16 * pair, b5o, n5o), 0, unroll=8)
    arrive("f5")
    parent = wq5[zp] + f5r[0].astype(f32)
    arrive("d6")
    for j in range(2):
        below = wq6[half + j]
        for k in range(3):
            below = below + d6r[k, j].astype(f32)
        g5v[j] = below.astype(bf16)

    def emit(level, size, first, ref):
        want = (16 * (leaf - 16 * first) + iota((16, 256), 0)).astype(f32)
        block = jnp.zeros((16, 16), f32)
        for s in range(size):
            block = block + mm_nt(hot(want == dl_[first + s][level - 1 : level]), ref[s])
        sep_out[0, level - 1] = block[0:8]
        sep_out[1, level - 1] = -block[8:16]

    own = parent - mm_nt(g5v[zp], blocks(n5, zp)) - mm_nt(g5v[1 - zp], blocks(n5o, zp))
    own = own.astype(bf16)
    now = xo[48:64] - mm_nt(own, b4[...])
    xo[48:64] = now
    for level in range(3, 0, -1):
        now = xo[16 * level - 16 : 16 * level] - mm_nt(now.astype(bf16), m123[level - 1])
        xo[16 * level - 16 : 16 * level] = now
    above = 16 * (dl - c + tgs[0, leaf])
    chosen = hot(iota((16, 256), 1) == above + iota((16, 256), 0))
    back = mm_nt(now.astype(bf16), chosen).astype(bf16)
    less = mm(back, eh[...])
    arrive("lw")
    mine = lwo[x]
    for k in range(3):
        mine = mine + lwr[k].astype(f32)
    leaf_out[0] = jnp.where(mask, mine[0] - less[:, 0:512], 0.0)
    leaf_out[1] = jnp.where(mask, mine[1] + less[:, 512:1024], 0.0)

    arrive("e6")
    for k in range(3):
        sixth = sixth + e6r[k].astype(f32)
    xo[64:80] = sixth
    xo[80:96] = (
        wn5[zp] + f5r[1].astype(f32)
        - mm_nt(g5v[zp], blocks(b5, zp)) - mm_nt(g5v[1 - zp], blocks(b5o, zp))
    )
    xo[96:128] = jnp.zeros((32, 256), f32)
    xt[...] = jnp.transpose(xo[...])
    start = pl.multiple_of(dl * 16, 16)
    turned = xt[pl.ds(start, 16), :]
    for row, level in enumerate((0, 1, 2, 3, 5, 4)):
        sep_out[0, level] = turned[0:8, 16 * row : 16 * row + 16]
        sep_out[1, level] = -turned[8:16, 16 * row : 16 * row + 16]
    arrive("g6")
    emit(7, 8, 0, g6g)

    for one in pending:
        one.wait_send()


def body(leaf_rhs, sep_rhs, leaf_inv, leaf_low, sep_inv, sep_low, leaf_live, targets):
    vm = pl.BlockSpec(memory_space=pltpu.VMEM)
    hb = pl.BlockSpec(memory_space=pltpu.HBM)
    sm = pl.BlockSpec(memory_space=pltpu.SMEM)
    V = pltpu.VMEM

    def rows(*lead):
        return V(lead + (16, 256), bf16)

    def squares(count):
        return V((count, 256, 256), bf16)

    out_leaf, out_sep = pl.pallas_call(
        kernel,
        out_shape=(
            jax.ShapeDtypeStruct((2, 16, 512), f32),
            jax.ShapeDtypeStruct((2, 7, 8, 16), f32),
        ),
        in_specs=[hb] * 7 + [sm],
        out_specs=(vm, vm),
        scratch_shapes=[
            V((2, 16, 512), f32), V((2, 7, 8, 16), f32), V((2, 128, 512), bf16),
            V((2, 8, 512), bf16), V((2, 8, 2032), bf16), V((2, 8, 1008), bf16),
            V((7, 128), jnp.int32), pltpu.SMEM((7, 128), jnp.int32),
            pltpu.SemaphoreType.DMA((8,)),
            V((16, 128), f32), V((16, 3072), f32), V((8, 2, 16, 128), bf16),
            V((8, 2, 16, 256), bf16), V((8, 2, 4, 16, 256), bf16),
            V((2, 16, 128), bf16), V((4, 16, 128), bf16), V((8, 16, 128), bf16), rows(4),
            V((4, 16, 128), bf16), V((4, 2, 16, 128), bf16),
            V((8, 2, 2, 16, 128), bf16), V((8, 2, 4, 16, 128), bf16), V((8, 2, 4, 2, 16, 128), bf16), V((8, 2, 2, 16, 128), bf16),
            V((4, 2, 16, 128), bf16), V((4, 2, 16, 128), bf16), V((16, 1024), bf16),
            V((8, 8, 256), f32), V((256, 256), bf16), squares(3),
            V((128, 256), f32), rows(4),
            squares(3), V((256, 256), bf16), rows(32), rows(64), rows(128), rows(32), rows(32),
            rows(32), rows(64), rows(128), squares(4), squares(2), squares(4),
            rows(8, 3), rows(2), rows(4), rows(8),
            V((4, 16, 256), f32), V((2, 16, 256), f32), V((4, 16, 256), f32), V((2, 16, 256), f32), rows(3), rows(3), rows(4), rows(3, 2), rows(2), rows(2),
            rows(8), rows(2),
            V((4, 2, 16, 512), bf16), V((3, 2, 16, 512), bf16), V((4, 2, 16, 512), f32),
            V((128, 256), f32), V((256, 128), f32),
            pltpu.SemaphoreType.DMA((COPIES,)), pltpu.SemaphoreType.DMA((COPIES,)),
        ],
        compiler_params=pltpu.CompilerParams(
            collective_id=0, has_side_effects=True, vmem_limit_bytes=40 * 2**20
        ),
    )(
        *(pltpu.with_memory_space_constraint(one, pltpu.HBM) for one in (
            leaf_rhs, sep_rhs.transpose(0, 2, 3, 1), leaf_inv, leaf_low.transpose(0, 2, 1),
            sep_inv, sep_low, targets,
        )),
        leaf_live,
    )
    return out_leaf, out_sep.transpose(0, 3, 1, 2)


def solution(mesh):
    placed = (
        P(None, "rhs", "leaf"),
        P(None, "rhs", None, "leaf"),
        P(None, "rhs", "leaf"),
        P(None, None, "leaf"),
        P(None, None, "leaf"),
        P(None, None, "leaf"),
        P("leaf"),
        P(),
    )
    return jax.shard_map(
        body,
        mesh=mesh,
        in_specs=placed,
        out_specs=(P(None, "rhs", "leaf"), P(None, "rhs", None, "leaf")),
        check_vma=False,
    )
```
